256 devices in a mesh: obs: 4 (over x_lo, core), pan: 64 (over x_hi, y, z).
Axes of the slice: x: 4 (x_hi: 2, x_lo: 2; x = x_hi * 2 + x_lo), y: 4, z: 8, core: 2. Of those that a mesh axis runs over, the one named last changes fastest.
Arguments:
- sources: bfloat16 [64, 4, 2048, 256], P('pan', None, 'obs'), may hold values from -16 to 16
- panel_places: float32 [64, 3, 2048], P('pan', None, 'obs'), may hold values from -8 to 8
- observer_places: float32 [3, 1024], P(None, 'obs'), may hold values from 20 to 60
- fraction: bfloat16 [1024, 64, 2048], P(None, 'pan', 'obs'), may hold values from 0 to 1
- delay_bins: int32 [8, 64, 16], P(None, 'pan', 'obs'), may hold values from 0 to 127
- segment_owner: int32 [64], replicated, may hold values from 0 to 63, each once
Outputs:
- pressure: float32 [384, 1024], P('pan', 'obs')
The draws below stay inside these ranges and needn't reach their ends.
Inputs may be any that keep to these rules, and one draw needn't show every extreme that they name: segment_owner is a permutation of the time segments' owners.
All inputs are finite; a program needn't handle non-finite values.
Results may differ from the reference program's by a relative error of at most 0.003.
Values may be sent and summed in bfloat16 or wider, within the bound.
A program may use at most 64 MiB of HBM per device.

```python
import math
import jax
import jax.numpy as jnp
from jax import lax

S = 256
MAXD = 127
OBLK = 128
PBLK = 128
OBS = 1024
TILE_PANELS = 2048
PANELS = 131072
TT = 384
SEGLEN = 6
NOB = 8
NBT = 16
N_PAN = 64


def with_ends(drawn, key, low, largest):
    extent = drawn.shape
    spot = [jax.random.randint(jax.random.fold_in(key, axis), (), 0, extent[axis]) for axis in range(len(extent))]
    drawn = drawn.at[tuple(spot)].set(low)
    longest = extent.index(max(extent))
    spot[longest] = (spot[longest] + 1) % extent[longest]
    return drawn.at[tuple(spot)].set(largest)


def strengthened(drawn, key, source, target, shards_of, factor):
    def block_of(axis_at):
        return (jnp.arange(drawn.shape[axis_at]) // (drawn.shape[axis_at] // shards_of)).reshape((-1,) + (1,) * (drawn.ndim - 1 - axis_at))

    near = jax.random.permutation(key, shards_of)[block_of(target)]
    second = (block_of(target) + shards_of // 2) % shards_of
    return jnp.where((block_of(source) == near) | (block_of(source) == second), factor * drawn, drawn)


def block_scale(key, extent, shards, low, high):
    def one(dim, parts):
        heights = jax.random.uniform(jax.random.fold_in(jax.random.fold_in(key, 6), dim), (parts,), jnp.float32, low / len(shards), high / len(shards))
        return jnp.repeat(jnp.exp(heights), extent[dim] // parts).reshape((-1,) + (1,) * (len(extent) - dim - 1))

    loudness = one(*shards[0])
    for cut in shards[1:]:
        loudness = loudness * one(*cut)
    return loudness


def noise_with(rng, dims, width, most, split, heavy, kind=jnp.bfloat16):
    values = width * jax.random.normal(rng, dims, jnp.float32)
    if split:
        values = values * block_scale(rng, dims, split, -0.22, 0.18)
    return jnp.clip(strengthened(values, jax.random.fold_in(rng, 3), *heavy), -most, most).astype(kind)


def setup_inputs(seed: int = 0) -> dict:
    key_list = jax.random.split(jax.random.key(seed), 7)
    sources = noise_with(key_list[0], (N_PAN, 4, TILE_PANELS, S), 1.0, 16.0, ((0, 64), (2, 4)), (0, 3, 64, 4.0))
    panel_places = jnp.clip(jax.random.uniform(key_list[1], (N_PAN, 3, TILE_PANELS), jnp.float32, -8.0, 8.0) * block_scale(key_list[1], (N_PAN, 3, TILE_PANELS), ((0, 64), (2, 4)), -0.4, 0.0), -8.0, 8.0)
    observer_places = jnp.clip(20.0 + 40.0 * jax.random.uniform(key_list[2], (3, OBS), jnp.float32) ** block_scale(key_list[2], (3, OBS), ((1, 4),), -0.2, 0.2), 20.0, 60.0)
    fraction = jnp.clip(1.0 * jax.random.uniform(key_list[3], (OBS, N_PAN, TILE_PANELS), jnp.float32) ** block_scale(key_list[3], (OBS, N_PAN, TILE_PANELS), ((1, 64), (2, 4)), -0.2, 0.2), 0.0, 1.0).astype(jnp.bfloat16)
    delay_bins = with_ends(jax.random.randint(key_list[4], (NOB, N_PAN, NBT), 0, MAXD + 1), jax.random.fold_in(key_list[4], 1), 0, MAXD).astype(jnp.int32)
    segment_owner = jax.random.permutation(key_list[5], N_PAN).astype(jnp.int32)
    return dict(sources=sources, panel_places=panel_places, observer_places=observer_places, fraction=fraction, delay_bins=delay_bins, segment_owner=segment_owner)


def reference(sources, panel_places, observer_places, fraction, delay_bins, segment_owner):
    amplitude = 60.0 / math.sqrt(PANELS)
    per_tile = TILE_PANELS // PBLK
    block_ids = jnp.arange(N_PAN * per_tile, dtype=jnp.int32)
    columns = jnp.broadcast_to(jnp.arange(OBS, dtype=jnp.int32)[None, :], (S + 1, OBS))
    steps_up = jnp.arange(S + 1, dtype=jnp.int32)[:, None]

    def step(totals, block_id):
        tile = (block_id // per_tile).astype(jnp.int32)
        inner = (block_id % per_tile * PBLK).astype(jnp.int32)
        zero = jnp.zeros((), jnp.int32)
        src_block = lax.dynamic_slice(sources, (tile, zero, inner, zero), (1, 4, PBLK, S))[0]
        place_block = lax.dynamic_slice(panel_places, (tile, zero, inner), (1, 3, PBLK))[0]
        frac_block = lax.dynamic_slice(fraction, (zero, tile, inner), (OBS, 1, PBLK))[:, 0]
        shifts = lax.dynamic_slice(delay_bins, (zero, tile, (block_id % per_tile).astype(jnp.int32)), (NOB, 1, 1))[:, 0, 0]
        separation = observer_places[:, :, None] - place_block[:, None, :]
        dist_sq = lax.optimization_barrier(jnp.sum(separation * separation, axis=0))
        monopole = amplitude / jnp.sqrt(dist_sq)
        dipole = amplitude * separation / dist_sq
        kernel = jnp.concatenate([monopole[None], dipole], axis=0)
        weight = frac_block.astype(jnp.float32)
        lower_part = (kernel * (1.0 - weight)).astype(jnp.bfloat16)
        upper_part = (kernel * weight).astype(jnp.bfloat16)
        stacked = jnp.stack([lower_part, upper_part], axis=0)
        products = jnp.einsum('cjs,gcoj->sgo', src_block.astype(jnp.float32), stacked.astype(jnp.float32))
        placed = jnp.pad(products[:, 0], ((0, 1), (0, 0))) + jnp.pad(products[:, 1], ((1, 0), (0, 0)))
        rows = jnp.repeat(shifts, OBLK).astype(jnp.int32)[None, :] + steps_up
        totals = totals.at[rows, columns].add(placed)
        return (totals, None)
    totals, _ = lax.scan(step, jnp.zeros((TT, OBS), jnp.float32), block_ids)
    segments = totals.reshape(N_PAN, SEGLEN, OBS)
    ordered = jnp.zeros_like(segments).at[segment_owner].set(segments)
    return ordered.reshape(TT, OBS)
```

```python
import math

import jax
import jax.numpy as jnp
from jax import lax
from jax.sharding import PartitionSpec as P

MAXD = 127
OBLK = 128
PBLK = 128


def block_kernel(place_block, observer_group, frac_group, amplitude):
    separation = observer_group[:, :, None] - place_block[:, None, :]
    dist_sq = jnp.sum(separation * separation, axis=0)
    monopole = amplitude / jnp.sqrt(dist_sq)
    dipole = amplitude * separation / dist_sq
    kernel = jnp.concatenate([monopole[None], dipole], axis=0)
    weight = frac_group.astype(jnp.float32)
    lower_part = (kernel * (1.0 - weight)).astype(jnp.bfloat16)
    upper_part = (kernel * weight).astype(jnp.bfloat16)
    return jnp.stack([lower_part, upper_part], axis=0)


def placed_block(src_block, weights):
    products = jnp.einsum("cjs,gcoj->sgo", src_block, weights, preferred_element_type=jnp.float32)
    return jnp.pad(products[:, 0], ((0, 1), (0, 0))) + jnp.pad(products[:, 1], ((1, 0), (0, 0)))


def per_device(sources, panel_places, observer_places, fraction, delay_bins, segment_owner):
    local_panels = sources.shape[2]
    window = sources.shape[3]
    bins_total = window + MAXD + 1
    amplitude = 60.0 / math.sqrt(local_panels * lax.axis_size("obs") * lax.axis_size("pan"))
    local_blocks = local_panels // PBLK
    every_obs = lax.all_gather(observer_places, "obs", axis=1, tiled=True)
    obs_total = every_obs.shape[1]
    obs_blocks = obs_total // OBLK
    span = window + 1
    lead = MAXD
    padded_rows = lead + span + (bins_total - span)
    columns = [None] * obs_blocks
    for block_index in range(local_blocks):
        lo_col = block_index * PBLK
        src_block = sources[0, :, lo_col : lo_col + PBLK]
        place_block = panel_places[0, :, lo_col : lo_col + PBLK]
        frac_cols = fraction[:, 0, lo_col : lo_col + PBLK]
        weights = block_kernel(place_block, every_obs, frac_cols, amplitude)
        placed = placed_block(src_block, weights)
        padded = jnp.pad(placed, ((lead, padded_rows - lead - span), (0, 0)))
        for ob in range(obs_blocks):
            shift = delay_bins[ob, 0, block_index]
            piece = lax.dynamic_slice(padded, (lead - shift, ob * OBLK), (bins_total, OBLK))
            columns[ob] = piece if columns[ob] is None else columns[ob] + piece
    totals = jnp.concatenate(columns, axis=1)
    reduced = lax.psum_scatter(totals, "obs", scatter_dimension=1, tiled=True)
    segment_count = segment_owner.shape[0]
    seg_len = bins_total // segment_count
    arranged = reduced.reshape(segment_count, seg_len, reduced.shape[1])
    inverse = jnp.argsort(segment_owner)
    arranged = arranged[inverse]
    rows = -(-seg_len // 8) * 8
    flat = jnp.pad(arranged, ((0, 0), (0, rows - seg_len), (0, 0)))
    result = lax.psum_scatter(flat, "pan", scatter_dimension=0, tiled=True)
    return result[0, :seg_len]


def solution(mesh):
    return jax.shard_map(
        per_device,
        mesh=mesh,
        in_specs=(
            P("pan", None, "obs", None),
            P("pan", None, "obs"),
            P(None, "obs"),
            P(None, "pan", "obs"),
            P(None, "pan", "obs"),
            P(),
        ),
        out_specs=P("pan", "obs"),
        check_vma=False,
    )
```

```python
import math

import jax
import jax.numpy as jnp
from jax import lax
from jax.sharding import PartitionSpec as P

MAXD = 127
OBLK = 128
PBLK = 128


def block_kernel(place_block, observer_group, frac_group, amplitude):
    separation = observer_group[:, :, None] - place_block[:, None, :]
    dist_sq = jnp.sum(separation * separation, axis=0)
    monopole = amplitude / jnp.sqrt(dist_sq)
    dipole = amplitude * separation / dist_sq
    kernel = jnp.concatenate([monopole[None], dipole], axis=0)
    weight = frac_group.astype(jnp.float32)
    lower_part = (kernel * (1.0 - weight)).astype(jnp.bfloat16)
    upper_part = (kernel * weight).astype(jnp.bfloat16)
    return jnp.stack([lower_part, upper_part], axis=0)


def placed_block(src_block, weights):
    products = jnp.einsum("cjs,gcoj->sgo", src_block, weights, preferred_element_type=jnp.float32)
    return jnp.pad(products[:, 0], ((0, 1), (0, 0))) + jnp.pad(products[:, 1], ((1, 0), (0, 0)))


def per_device(sources, panel_places, observer_places, fraction, delay_bins, segment_owner):
    local_panels = sources.shape[2]
    window = sources.shape[3]
    bins_total = window + MAXD + 1
    amplitude = 60.0 / math.sqrt(local_panels * lax.axis_size("obs") * lax.axis_size("pan"))
    local_blocks = local_panels // PBLK
    every_obs = lax.all_gather(observer_places, "obs", axis=1, tiled=True)
    obs_total = every_obs.shape[1]
    obs_blocks = obs_total // OBLK
    span = window + 1
    lead = MAXD
    padded_rows = lead + span + (bins_total - span)
    columns = [None] * obs_blocks
    for block_index in range(local_blocks):
        lo_col = block_index * PBLK
        src_block = sources[0, :, lo_col : lo_col + PBLK]
        place_block = panel_places[0, :, lo_col : lo_col + PBLK]
        frac_cols = fraction[:, 0, lo_col : lo_col + PBLK]
        weights = block_kernel(place_block, every_obs, frac_cols, amplitude)
        placed = placed_block(src_block, weights)
        padded = jnp.pad(placed, ((lead, padded_rows - lead - span), (0, 0)))
        for ob in range(obs_blocks):
            shift = delay_bins[ob, 0, block_index]
            piece = lax.dynamic_slice(padded, (lead - shift, ob * OBLK), (bins_total, OBLK))
            columns[ob] = piece if columns[ob] is None else columns[ob] + piece
    totals = jnp.concatenate(columns, axis=1)
    reduced = lax.psum_scatter(totals, "obs", scatter_dimension=1, tiled=True)
    segment_count = segment_owner.shape[0]
    seg_len = bins_total // segment_count
    arranged = reduced.reshape(segment_count, seg_len, reduced.shape[1])
    inverse = jnp.argsort(segment_owner)
    arranged = arranged[inverse]
    return halving_sum(arranged, "pan", (0, 3, 1, 4, 2, 5))


def halving_sum(data, axis, bit_order):
    count = data.shape[0]
    levels = count.bit_length() - 1
    me = lax.axis_index(axis)
    data = data.reshape((2,) * levels + data.shape[1:])
    remaining = list(range(levels - 1, -1, -1))
    for bit in bit_order:
        dim = remaining.index(bit)
        mine = (me >> bit) & 1
        low = lax.index_in_dim(data, 0, dim, keepdims=False)
        high = lax.index_in_dim(data, 1, dim, keepdims=False)
        keep = jnp.where(mine == 1, high, low)
        send = jnp.where(mine == 1, low, high)
        pairs = [(p, p ^ (1 << bit)) for p in range(count)]
        data = keep + lax.ppermute(send, axis, pairs)
        remaining.pop(dim)
    return data


def solution(mesh):
    return jax.shard_map(
        per_device,
        mesh=mesh,
        in_specs=(
            P("pan", None, "obs", None),
            P("pan", None, "obs"),
            P(None, "obs"),
            P(None, "pan", "obs"),
            P(None, "pan", "obs"),
            P(),
        ),
        out_specs=P("pan", "obs"),
        check_vma=False,
    )
```

```python
import functools
import math

import jax
import jax.numpy as jnp
from jax import lax
from jax.experimental import pallas as pl
from jax.experimental.pallas import tpu as pltpu
from jax.sharding import PartitionSpec as P

MAXD = 127
OBLK = 128
PBLK = 128


def fwh_kernel(bins_ref, obs_ref, place_ref, frac_ref, src_ref, out_ref, *, amplitude, panel_blocks, window, bins_total):
    ob = pl.program_id(0)
    acc = jnp.zeros((OBLK, bins_total), jnp.float32)
    pad = jnp.zeros((OBLK, bins_total - window), jnp.float32)
    for pb in range(panel_blocks):
        cols = slice(pb * PBLK, (pb + 1) * PBLK)
        seps = [obs_ref[:, c : c + 1] - place_ref[c : c + 1, cols] for c in range(3)]
        dist_sq = seps[0] * seps[0] + seps[1] * seps[1] + seps[2] * seps[2]
        parts = [amplitude / jnp.sqrt(dist_sq)] + [amplitude * sep / dist_sq for sep in seps]
        weight = frac_ref[:, cols].astype(jnp.float32)
        low = None
        high = None
        for c in range(4):
            src = src_ref[c, cols, :]
            lo_w = (parts[c] * (1.0 - weight)).astype(jnp.bfloat16)
            hi_w = (parts[c] * weight).astype(jnp.bfloat16)
            lo_p = jnp.dot(lo_w, src, preferred_element_type=jnp.float32)
            hi_p = jnp.dot(hi_w, src, preferred_element_type=jnp.float32)
            low = lo_p if low is None else low + lo_p
            high = hi_p if high is None else high + hi_p
        shift = bins_ref[ob, pb]
        acc = acc + pltpu.roll(jnp.concatenate([low, pad], axis=1), shift, 1)
        acc = acc + pltpu.roll(jnp.concatenate([high, pad], axis=1), shift + 1, 1)
    out_ref[...] = acc.T


def per_device(sources, panel_places, observer_places, fraction, delay_bins, segment_owner):
    local_panels = sources.shape[2]
    window = sources.shape[3]
    bins_total = window + MAXD + 1
    amplitude = 60.0 / math.sqrt(local_panels * lax.axis_size("obs") * lax.axis_size("pan"))
    panel_blocks = local_panels // PBLK
    every_obs = lax.all_gather(observer_places, "obs", axis=1, tiled=True)
    obs_total = every_obs.shape[1]
    obs_blocks = obs_total // OBLK
    kernel = functools.partial(fwh_kernel, amplitude=amplitude, panel_blocks=panel_blocks, window=window, bins_total=bins_total)
    grid_spec = pltpu.PrefetchScalarGridSpec(
        num_scalar_prefetch=1,
        grid=(obs_blocks,),
        in_specs=[
            pl.BlockSpec((OBLK, 3), lambda i, b: (i, 0)),
            pl.BlockSpec((3, local_panels), lambda i, b: (0, 0)),
            pl.BlockSpec((OBLK, local_panels), lambda i, b: (i, 0)),
            pl.BlockSpec((4, local_panels, window), lambda i, b: (0, 0, 0)),
        ],
        out_specs=pl.BlockSpec((bins_total, OBLK), lambda i, b: (0, i)),
    )
    totals = pl.pallas_call(
        kernel,
        grid_spec=grid_spec,
        out_shape=jax.ShapeDtypeStruct((bins_total, obs_total), jnp.float32),
    )(delay_bins[:, 0, :], every_obs.T, panel_places[0], fraction[:, 0, :], sources[0])
    reduced = lax.psum_scatter(totals, "obs", scatter_dimension=1, tiled=True)
    segment_count = segment_owner.shape[0]
    seg_len = bins_total // segment_count
    arranged = reduced.reshape(segment_count, seg_len, reduced.shape[1])
    inverse = jnp.argsort(segment_owner)
    arranged = arranged[inverse]
    return halving_sum(arranged, "pan", (0, 3, 1, 4, 2, 5))


def halving_sum(data, axis, bit_order):
    count = data.shape[0]
    levels = count.bit_length() - 1
    me = lax.axis_index(axis)
    data = data.reshape((2,) * levels + data.shape[1:])
    remaining = list(range(levels - 1, -1, -1))
    for bit in bit_order:
        dim = remaining.index(bit)
        mine = (me >> bit) & 1
        low = lax.index_in_dim(data, 0, dim, keepdims=False)
        high = lax.index_in_dim(data, 1, dim, keepdims=False)
        keep = jnp.where(mine == 1, high, low)
        send = jnp.where(mine == 1, low, high)
        pairs = [(p, p ^ (1 << bit)) for p in range(count)]
        data = keep + lax.ppermute(send, axis, pairs)
        remaining.pop(dim)
    return data


def solution(mesh):
    return jax.shard_map(
        per_device,
        mesh=mesh,
        in_specs=(
            P("pan", None, "obs", None),
            P("pan", None, "obs"),
            P(None, "obs"),
            P(None, "pan", "obs"),
            P(None, "pan", "obs"),
            P(),
        ),
        out_specs=P("pan", "obs"),
        check_vma=False,
    )
```

```python
import functools
import math

import jax
import jax.numpy as jnp
from jax import lax
from jax.experimental import pallas as pl
from jax.experimental.pallas import tpu as pltpu
from jax.sharding import PartitionSpec as P

MAXD = 127
OBLK = 128
PBLK = 128


def fwh_kernel(bins_ref, obs_ref, place_ref, frac_ref, src_ref, out_ref, *, amplitude, panel_blocks, window, bins_total):
    ob = pl.program_id(0)
    acc = jnp.zeros((OBLK, bins_total), jnp.float32)
    pad = jnp.zeros((OBLK, bins_total - window), jnp.float32)
    for pb in range(panel_blocks):
        cols = slice(pb * PBLK, (pb + 1) * PBLK)
        seps = [obs_ref[:, c : c + 1] - place_ref[c : c + 1, cols] for c in range(3)]
        dist_sq = seps[0] * seps[0] + seps[1] * seps[1] + seps[2] * seps[2]
        parts = [amplitude / jnp.sqrt(dist_sq)] + [amplitude * sep / dist_sq for sep in seps]
        weight = frac_ref[:, cols].astype(jnp.float32)
        low = None
        high = None
        for c in range(4):
            src = src_ref[c, cols, :]
            lo_w = (parts[c] * (1.0 - weight)).astype(jnp.bfloat16)
            hi_w = (parts[c] * weight).astype(jnp.bfloat16)
            lo_p = jnp.dot(lo_w, src, preferred_element_type=jnp.float32)
            hi_p = jnp.dot(hi_w, src, preferred_element_type=jnp.float32)
            low = lo_p if low is None else low + lo_p
            high = hi_p if high is None else high + hi_p
        shift = bins_ref[ob, pb]
        acc = acc + pltpu.roll(jnp.concatenate([low, pad], axis=1), shift, 1)
        acc = acc + pltpu.roll(jnp.concatenate([high, pad], axis=1), shift + 1, 1)
    out_ref[...] = acc.T


def per_device(sources, panel_places, observer_places, fraction, delay_bins, segment_owner):
    local_panels = sources.shape[2]
    window = sources.shape[3]
    bins_total = window + MAXD + 1
    amplitude = 60.0 / math.sqrt(local_panels * lax.axis_size("obs") * lax.axis_size("pan"))
    panel_blocks = local_panels // PBLK
    every_obs = lax.all_gather(observer_places, "obs", axis=1, tiled=True)
    obs_total = every_obs.shape[1]
    obs_blocks = obs_total // OBLK
    kernel = functools.partial(fwh_kernel, amplitude=amplitude, panel_blocks=panel_blocks, window=window, bins_total=bins_total)
    grid_spec = pltpu.PrefetchScalarGridSpec(
        num_scalar_prefetch=1,
        grid=(obs_blocks,),
        in_specs=[
            pl.BlockSpec((OBLK, 3), lambda i, b: (i, 0)),
            pl.BlockSpec((3, local_panels), lambda i, b: (0, 0)),
            pl.BlockSpec((OBLK, local_panels), lambda i, b: (i, 0)),
            pl.BlockSpec((4, local_panels, window), lambda i, b: (0, 0, 0)),
        ],
        out_specs=pl.BlockSpec((bins_total, OBLK), lambda i, b: (0, i)),
    )
    totals = pl.pallas_call(
        kernel,
        grid_spec=grid_spec,
        out_shape=jax.ShapeDtypeStruct((bins_total, obs_total), jnp.float32),
    )(delay_bins[:, 0, :], every_obs.T, panel_places[0], fraction[:, 0, :], sources[0])
    quarter = obs_total // 4
    halves = totals.reshape(bins_total, 2, 2, quarter)
    me = lax.axis_index("obs")
    for bit, dim in ((0, 2), (1, 1)):
        mine = (me >> bit) & 1
        low = lax.index_in_dim(halves, 0, dim, keepdims=False)
        high = lax.index_in_dim(halves, 1, dim, keepdims=False)
        keep = jnp.where(mine == 1, high, low)
        send = jnp.where(mine == 1, low, high)
        pairs = [(p, p ^ (1 << bit)) for p in range(4)]
        halves = keep + lax.ppermute(send, "obs", pairs)
    reduced = halves
    segment_count = segment_owner.shape[0]
    seg_len = bins_total // segment_count
    arranged = reduced.reshape(segment_count, seg_len, reduced.shape[1])
    inverse = jnp.argsort(segment_owner)
    arranged = arranged[inverse]
    return halving_sum(arranged, "pan", (0, 3, 1, 4, 2, 5))


def halving_sum(data, axis, bit_order):
    count = data.shape[0]
    levels = count.bit_length() - 1
    me = lax.axis_index(axis)
    data = data.reshape((2,) * levels + data.shape[1:])
    remaining = list(range(levels - 1, -1, -1))
    for bit in bit_order:
        dim = remaining.index(bit)
        mine = (me >> bit) & 1
        low = lax.index_in_dim(data, 0, dim, keepdims=False)
        high = lax.index_in_dim(data, 1, dim, keepdims=False)
        keep = jnp.where(mine == 1, high, low)
        send = jnp.where(mine == 1, low, high)
        pairs = [(p, p ^ (1 << bit)) for p in range(count)]
        data = keep + lax.ppermute(send, axis, pairs)
        remaining.pop(dim)
    return data


def solution(mesh):
    return jax.shard_map(
        per_device,
        mesh=mesh,
        in_specs=(
            P("pan", None, "obs", None),
            P("pan", None, "obs"),
            P(None, "obs"),
            P(None, "pan", "obs"),
            P(None, "pan", "obs"),
            P(),
        ),
        out_specs=P("pan", "obs"),
        check_vma=False,
    )
```

```python
import functools
import math

import jax
import jax.numpy as jnp
from jax import lax
from jax.experimental import pallas as pl
from jax.experimental.pallas import tpu as pltpu
from jax.sharding import PartitionSpec as P

MAXD = 127
OBLK = 128
PBLK = 128


def fwh_kernel(bins_ref, obs_ref, place_ref, frac_ref, src_ref, out_ref, *, amplitude, panel_blocks, window, bins_total):
    ob = pl.program_id(0)
    acc = jnp.zeros((OBLK, bins_total), jnp.float32)
    pad = jnp.zeros((OBLK, bins_total - window), jnp.float32)
    for pb in range(panel_blocks):
        cols = slice(pb * PBLK, (pb + 1) * PBLK)
        seps = [obs_ref[:, c : c + 1] - place_ref[c : c + 1, cols] for c in range(3)]
        dist_sq = seps[0] * seps[0] + seps[1] * seps[1] + seps[2] * seps[2]
        parts = [amplitude / jnp.sqrt(dist_sq)] + [amplitude * sep / dist_sq for sep in seps]
        weight = frac_ref[:, cols].astype(jnp.float32)
        low = None
        high = None
        for c in range(4):
            src = src_ref[c, cols, :]
            lo_w = (parts[c] * (1.0 - weight)).astype(jnp.bfloat16)
            hi_w = (parts[c] * weight).astype(jnp.bfloat16)
            lo_p = jnp.dot(lo_w, src, preferred_element_type=jnp.float32)
            hi_p = jnp.dot(hi_w, src, preferred_element_type=jnp.float32)
            low = lo_p if low is None else low + lo_p
            high = hi_p if high is None else high + hi_p
        shift = bins_ref[ob, pb]
        acc = acc + pltpu.roll(jnp.concatenate([low, pad], axis=1), shift, 1)
        acc = acc + pltpu.roll(jnp.concatenate([high, pad], axis=1), shift + 1, 1)
    out_ref[...] = acc.T


def per_device(sources, panel_places, observer_places, fraction, delay_bins, segment_owner):
    local_panels = sources.shape[2]
    window = sources.shape[3]
    bins_total = window + MAXD + 1
    amplitude = 60.0 / math.sqrt(local_panels * lax.axis_size("obs") * lax.axis_size("pan"))
    panel_blocks = local_panels // PBLK
    every_obs = lax.all_gather(observer_places, "obs", axis=1, tiled=True)
    obs_total = every_obs.shape[1]
    obs_blocks = obs_total // OBLK
    kernel = functools.partial(fwh_kernel, amplitude=amplitude, panel_blocks=panel_blocks, window=window, bins_total=bins_total)
    grid_spec = pltpu.PrefetchScalarGridSpec(
        num_scalar_prefetch=1,
        grid=(obs_blocks,),
        in_specs=[
            pl.BlockSpec((OBLK, 3), lambda i, b: (i, 0)),
            pl.BlockSpec((3, local_panels), lambda i, b: (0, 0)),
            pl.BlockSpec((OBLK, local_panels), lambda i, b: (i, 0)),
            pl.BlockSpec((4, local_panels, window), lambda i, b: (0, 0, 0)),
        ],
        out_specs=pl.BlockSpec((None, bins_total, OBLK), lambda i, b: (i // 2, 0, i % 2)),
    )
    totals = pl.pallas_call(
        kernel,
        grid_spec=grid_spec,
        out_shape=jax.ShapeDtypeStruct((obs_blocks // 2, bins_total, 2 * OBLK), jnp.float32),
    )(delay_bins[:, 0, :], every_obs.T, panel_places[0], fraction[:, 0, :], sources[0])
    halves = totals.reshape((2, 2) + totals.shape[1:])
    me = lax.axis_index("obs")
    for bit, dim in ((0, 1), (1, 0)):
        mine = (me >> bit) & 1
        low = lax.index_in_dim(halves, 0, dim, keepdims=False)
        high = lax.index_in_dim(halves, 1, dim, keepdims=False)
        keep = jnp.where(mine == 1, high, low)
        send = jnp.where(mine == 1, low, high)
        pairs = [(p, p ^ (1 << bit)) for p in range(4)]
        halves = keep + lax.ppermute(send, "obs", pairs)
    reduced = halves
    segment_count = segment_owner.shape[0]
    seg_len = bins_total // segment_count
    arranged = reduced.reshape(segment_count, seg_len, reduced.shape[1])
    inverse = jnp.argsort(segment_owner)
    arranged = arranged[inverse]
    return halving_sum(arranged, "pan", (0, 3, 1, 4, 2, 5))


def halving_sum(data, axis, bit_order):
    count = data.shape[0]
    levels = count.bit_length() - 1
    me = lax.axis_index(axis)
    data = data.reshape((2,) * levels + data.shape[1:])
    remaining = list(range(levels - 1, -1, -1))
    for bit in bit_order:
        dim = remaining.index(bit)
        mine = (me >> bit) & 1
        low = lax.index_in_dim(data, 0, dim, keepdims=False)
        high = lax.index_in_dim(data, 1, dim, keepdims=False)
        keep = jnp.where(mine == 1, high, low)
        send = jnp.where(mine == 1, low, high)
        pairs = [(p, p ^ (1 << bit)) for p in range(count)]
        data = keep + lax.ppermute(send, axis, pairs)
        remaining.pop(dim)
    return data


def solution(mesh):
    return jax.shard_map(
        per_device,
        mesh=mesh,
        in_specs=(
            P("pan", None, "obs", None),
            P("pan", None, "obs"),
            P(None, "obs"),
            P(None, "pan", "obs"),
            P(None, "pan", "obs"),
            P(),
        ),
        out_specs=P("pan", "obs"),
        check_vma=False,
    )
```

```python
import functools
import math

import jax
import jax.numpy as jnp
from jax import lax
from jax.experimental import pallas as pl
from jax.experimental.pallas import tpu as pltpu
from jax.sharding import PartitionSpec as P

MAXD = 127
OBLK = 128
PBLK = 128


def fwh_kernel(bins_ref, obs_ref, place_ref, frac_ref, src_ref, out_ref, *, amplitude, panel_blocks, window, bins_total):
    ob = pl.program_id(0)
    acc = jnp.zeros((OBLK, bins_total), jnp.float32)
    pad = jnp.zeros((OBLK, bins_total - window), jnp.float32)
    for pb in range(panel_blocks):
        cols = slice(pb * PBLK, (pb + 1) * PBLK)
        seps = [obs_ref[:, c : c + 1] - place_ref[c : c + 1, cols] for c in range(3)]
        dist_sq = seps[0] * seps[0] + seps[1] * seps[1] + seps[2] * seps[2]
        parts = [amplitude / jnp.sqrt(dist_sq)] + [amplitude * sep / dist_sq for sep in seps]
        weight = frac_ref[:, cols].astype(jnp.float32)
        low = None
        high = None
        for c in range(4):
            src = src_ref[c, cols, :]
            lo_w = (parts[c] * (1.0 - weight)).astype(jnp.bfloat16)
            hi_w = (parts[c] * weight).astype(jnp.bfloat16)
            lo_p = jnp.dot(lo_w, src, preferred_element_type=jnp.float32)
            hi_p = jnp.dot(hi_w, src, preferred_element_type=jnp.float32)
            low = lo_p if low is None else low + lo_p
            high = hi_p if high is None else high + hi_p
        shift = bins_ref[ob, pb]
        acc = acc + pltpu.roll(jnp.concatenate([low, pad], axis=1), shift, 1)
        acc = acc + pltpu.roll(jnp.concatenate([high, pad], axis=1), shift + 1, 1)
    out_ref[...] = acc.T


def per_device(sources, panel_places, observer_places, fraction, delay_bins, segment_owner):
    local_panels = sources.shape[2]
    window = sources.shape[3]
    bins_total = window + MAXD + 1
    amplitude = 60.0 / math.sqrt(local_panels * lax.axis_size("obs") * lax.axis_size("pan"))
    panel_blocks = local_panels // PBLK
    every_obs = lax.all_gather(observer_places, "obs", axis=1, tiled=True)
    obs_total = every_obs.shape[1]
    obs_blocks = obs_total // OBLK
    kernel = functools.partial(fwh_kernel, amplitude=amplitude, panel_blocks=panel_blocks, window=window, bins_total=bins_total)
    grid_spec = pltpu.PrefetchScalarGridSpec(
        num_scalar_prefetch=1,
        grid=(obs_blocks,),
        in_specs=[
            pl.BlockSpec((OBLK, 3), lambda i, b: (i, 0)),
            pl.BlockSpec((3, local_panels), lambda i, b: (0, 0)),
            pl.BlockSpec((OBLK, local_panels), lambda i, b: (i, 0)),
            pl.BlockSpec((4, local_panels, window), lambda i, b: (0, 0, 0)),
        ],
        out_specs=pl.BlockSpec((None, bins_total, OBLK), lambda i, b: (i // 2, 0, i % 2)),
    )
    totals = pl.pallas_call(
        kernel,
        grid_spec=grid_spec,
        out_shape=jax.ShapeDtypeStruct((obs_blocks // 2, bins_total, 2 * OBLK), jnp.float32),
    )(delay_bins[:, 0, :], every_obs.T, panel_places[0], fraction[:, 0, :], sources[0])
    halves = totals.reshape((2, 2) + totals.shape[1:])
    me = lax.axis_index("obs")
    for bit, dim in ((0, 1), (1, 0)):
        mine = (me >> bit) & 1
        low = lax.index_in_dim(halves, 0, dim, keepdims=False)
        high = lax.index_in_dim(halves, 1, dim, keepdims=False)
        keep = jnp.where(mine == 1, high, low)
        send = jnp.where(mine == 1, low, high)
        pairs = [(p, p ^ (1 << bit)) for p in range(4)]
        halves = keep + lax.ppermute(send, "obs", pairs)
    reduced = halves
    segment_count = segment_owner.shape[0]
    seg_len = bins_total // segment_count
    arranged = reduced.reshape(segment_count, seg_len, reduced.shape[1])
    inverse = jnp.argsort(segment_owner)
    arranged = arranged[inverse]
    gathered = lax.all_to_all(arranged, "pan", 0, 0, tiled=True)
    return jnp.sum(gathered, axis=0)


def halving_sum(data, axis, bit_order):
    count = data.shape[0]
    levels = count.bit_length() - 1
    me = lax.axis_index(axis)
    data = data.reshape((2,) * levels + data.shape[1:])
    remaining = list(range(levels - 1, -1, -1))
    for bit in bit_order:
        dim = remaining.index(bit)
        mine = (me >> bit) & 1
        low = lax.index_in_dim(data, 0, dim, keepdims=False)
        high = lax.index_in_dim(data, 1, dim, keepdims=False)
        keep = jnp.where(mine == 1, high, low)
        send = jnp.where(mine == 1, low, high)
        pairs = [(p, p ^ (1 << bit)) for p in range(count)]
        data = keep + lax.ppermute(send, axis, pairs)
        remaining.pop(dim)
    return data


def solution(mesh):
    return jax.shard_map(
        per_device,
        mesh=mesh,
        in_specs=(
            P("pan", None, "obs", None),
            P("pan", None, "obs"),
            P(None, "obs"),
            P(None, "pan", "obs"),
            P(None, "pan", "obs"),
            P(),
        ),
        out_specs=P("pan", "obs"),
        check_vma=False,
    )
```

```python
import functools
import math

import jax
import jax.numpy as jnp
from jax import lax
from jax.experimental import pallas as pl
from jax.experimental.pallas import tpu as pltpu
from jax.sharding import PartitionSpec as P

MAXD = 127
OBLK = 128
PBLK = 128


def fwh_kernel(bins_ref, obs_ref, place_ref, frac_ref, src_ref, out_ref, *, amplitude, panel_blocks, window, bins_total):
    ob = pl.program_id(0)
    acc = jnp.zeros((OBLK, bins_total), jnp.float32)
    pad = jnp.zeros((OBLK, bins_total - window), jnp.float32)
    for pb in range(panel_blocks):
        cols = slice(pb * PBLK, (pb + 1) * PBLK)
        seps = [obs_ref[:, c : c + 1] - place_ref[c : c + 1, cols] for c in range(3)]
        dist_sq = seps[0] * seps[0] + seps[1] * seps[1] + seps[2] * seps[2]
        parts = [amplitude / jnp.sqrt(dist_sq)] + [amplitude * sep / dist_sq for sep in seps]
        weight = frac_ref[:, cols].astype(jnp.float32)
        low = None
        high = None
        for c in range(4):
            src = src_ref[c, cols, :]
            lo_w = (parts[c] * (1.0 - weight)).astype(jnp.bfloat16)
            hi_w = (parts[c] * weight).astype(jnp.bfloat16)
            lo_p = jnp.dot(lo_w, src, preferred_element_type=jnp.float32)
            hi_p = jnp.dot(hi_w, src, preferred_element_type=jnp.float32)
            low = lo_p if low is None else low + lo_p
            high = hi_p if high is None else high + hi_p
        shift = bins_ref[ob, pb]
        acc = acc + pltpu.roll(jnp.concatenate([low, pad], axis=1), shift, 1)
        acc = acc + pltpu.roll(jnp.concatenate([high, pad], axis=1), shift + 1, 1)
    out_ref[...] = acc.T


def per_device(sources, panel_places, observer_places, fraction, delay_bins, segment_owner):
    local_panels = sources.shape[2]
    window = sources.shape[3]
    bins_total = window + MAXD + 1
    amplitude = 60.0 / math.sqrt(local_panels * lax.axis_size("obs") * lax.axis_size("pan"))
    panel_blocks = local_panels // PBLK
    every_obs = lax.all_gather(observer_places, "obs", axis=1, tiled=True)
    obs_total = every_obs.shape[1]
    obs_blocks = obs_total // OBLK
    kernel = functools.partial(fwh_kernel, amplitude=amplitude, panel_blocks=panel_blocks, window=window, bins_total=bins_total)
    grid_spec = pltpu.PrefetchScalarGridSpec(
        num_scalar_prefetch=1,
        grid=(obs_blocks,),
        in_specs=[
            pl.BlockSpec((OBLK, 3), lambda i, b: (i, 0)),
            pl.BlockSpec((3, local_panels), lambda i, b: (0, 0)),
            pl.BlockSpec((OBLK, local_panels), lambda i, b: (i, 0)),
            pl.BlockSpec((4, local_panels, window), lambda i, b: (0, 0, 0)),
        ],
        out_specs=pl.BlockSpec((None, bins_total, OBLK), lambda i, b: (i // 2, 0, i % 2)),
    )
    totals = pl.pallas_call(
        kernel,
        grid_spec=grid_spec,
        out_shape=jax.ShapeDtypeStruct((obs_blocks // 2, bins_total, 2 * OBLK), jnp.float32),
    )(delay_bins[:, 0, :], every_obs.T, panel_places[0], fraction[:, 0, :], sources[0])
    halves = totals.reshape((2, 2) + totals.shape[1:])
    me = lax.axis_index("obs")
    for bit, dim in ((0, 1), (1, 0)):
        mine = (me >> bit) & 1
        low = lax.index_in_dim(halves, 0, dim, keepdims=False)
        high = lax.index_in_dim(halves, 1, dim, keepdims=False)
        keep = jnp.where(mine == 1, high, low)
        send = jnp.where(mine == 1, low, high)
        pairs = [(p, p ^ (1 << bit)) for p in range(4)]
        halves = keep + lax.ppermute(send, "obs", pairs)
    reduced = halves
    segment_count = segment_owner.shape[0]
    seg_len = bins_total // segment_count
    arranged = reduced.reshape(segment_count, seg_len, reduced.shape[1])
    inverse = jnp.argsort(segment_owner)
    arranged = arranged[inverse]
    rows = -(-seg_len // 8) * 8
    padded = jnp.pad(arranged, ((0, 0), (0, rows - seg_len), (0, 0)))
    return exchange_sum(padded)[:seg_len]


def exchange_kernel(x_ref, out_ref, slots, send_sem, recv_sem):
    count = x_ref.shape[0]
    me = lax.axis_index("pan")

    def send(d, carry):
        target = lax.rem(me + d, count)
        pltpu.make_async_remote_copy(
            src_ref=x_ref.at[target],
            dst_ref=slots.at[me],
            send_sem=send_sem.at[target],
            recv_sem=recv_sem.at[me],
            device_id={"pan": target},
            device_id_type=pl.DeviceIdType.MESH,
        ).start()
        return carry

    lax.fori_loop(1, count, send, 0)
    total = x_ref[me]

    def gather(d, total):
        source = lax.rem(me + count - d, count)
        pltpu.make_async_remote_copy(
            src_ref=x_ref.at[source],
            dst_ref=slots.at[source],
            send_sem=send_sem.at[source],
            recv_sem=recv_sem.at[source],
            device_id={"pan": source},
            device_id_type=pl.DeviceIdType.MESH,
        ).wait_recv()
        return total + slots[source]

    total = lax.fori_loop(1, count, gather, total)

    def drain(d, carry):
        target = lax.rem(me + d, count)
        pltpu.make_async_remote_copy(
            src_ref=x_ref.at[target],
            dst_ref=slots.at[me],
            send_sem=send_sem.at[target],
            recv_sem=recv_sem.at[me],
            device_id={"pan": target},
            device_id_type=pl.DeviceIdType.MESH,
        ).wait_send()
        return carry

    lax.fori_loop(1, count, drain, 0)
    out_ref[...] = total


def exchange_sum(data):
    count = data.shape[0]
    return pl.pallas_call(
        exchange_kernel,
        out_shape=jax.ShapeDtypeStruct(data.shape[1:], data.dtype),
        in_specs=[pl.BlockSpec(memory_space=pltpu.VMEM)],
        out_specs=pl.BlockSpec(memory_space=pltpu.VMEM),
        scratch_shapes=[
            pltpu.VMEM(data.shape, data.dtype),
            pltpu.SemaphoreType.DMA((count,)),
            pltpu.SemaphoreType.DMA((count,)),
        ],
        compiler_params=pltpu.CompilerParams(has_side_effects=True),
    )(data)


def halving_sum(data, axis, bit_order):
    count = data.shape[0]
    levels = count.bit_length() - 1
    me = lax.axis_index(axis)
    data = data.reshape((2,) * levels + data.shape[1:])
    remaining = list(range(levels - 1, -1, -1))
    for bit in bit_order:
        dim = remaining.index(bit)
        mine = (me >> bit) & 1
        low = lax.index_in_dim(data, 0, dim, keepdims=False)
        high = lax.index_in_dim(data, 1, dim, keepdims=False)
        keep = jnp.where(mine == 1, high, low)
        send = jnp.where(mine == 1, low, high)
        pairs = [(p, p ^ (1 << bit)) for p in range(count)]
        data = keep + lax.ppermute(send, axis, pairs)
        remaining.pop(dim)
    return data


def solution(mesh):
    return jax.shard_map(
        per_device,
        mesh=mesh,
        in_specs=(
            P("pan", None, "obs", None),
            P("pan", None, "obs"),
            P(None, "obs"),
            P(None, "pan", "obs"),
            P(None, "pan", "obs"),
            P(),
        ),
        out_specs=P("pan", "obs"),
        check_vma=False,
    )
```

```python
import functools
import math

import jax
import jax.numpy as jnp
from jax import lax
from jax.experimental import pallas as pl
from jax.experimental.pallas import tpu as pltpu
from jax.sharding import PartitionSpec as P

MAXD = 127
OBLK = 128
PBLK = 128


def fwh_kernel(bins_ref, obs_ref, place_ref, frac_ref, src_ref, out_ref, *, amplitude, panel_blocks, window, bins_total):
    ob = pl.program_id(0)
    acc = jnp.zeros((OBLK, bins_total), jnp.float32)
    pad = jnp.zeros((OBLK, bins_total - window), jnp.float32)
    for pb in range(panel_blocks):
        cols = slice(pb * PBLK, (pb + 1) * PBLK)
        seps = [obs_ref[:, c : c + 1] - place_ref[c : c + 1, cols] for c in range(3)]
        dist_sq = seps[0] * seps[0] + seps[1] * seps[1] + seps[2] * seps[2]
        parts = [amplitude / jnp.sqrt(dist_sq)] + [amplitude * sep / dist_sq for sep in seps]
        weight = frac_ref[:, cols].astype(jnp.float32)
        low = None
        high = None
        for c in range(4):
            src = src_ref[c, cols, :]
            lo_w = (parts[c] * (1.0 - weight)).astype(jnp.bfloat16)
            hi_w = (parts[c] * weight).astype(jnp.bfloat16)
            lo_p = jnp.dot(lo_w, src, preferred_element_type=jnp.float32)
            hi_p = jnp.dot(hi_w, src, preferred_element_type=jnp.float32)
            low = lo_p if low is None else low + lo_p
            high = hi_p if high is None else high + hi_p
        shift = bins_ref[ob, pb]
        acc = acc + pltpu.roll(jnp.concatenate([low, pad], axis=1), shift, 1)
        acc = acc + pltpu.roll(jnp.concatenate([high, pad], axis=1), shift + 1, 1)
    out_ref[...] = acc.T


def per_device(sources, panel_places, observer_places, fraction, delay_bins, segment_owner):
    local_panels = sources.shape[2]
    window = sources.shape[3]
    bins_total = window + MAXD + 1
    amplitude = 60.0 / math.sqrt(local_panels * lax.axis_size("obs") * lax.axis_size("pan"))
    panel_blocks = local_panels // PBLK
    every_obs = lax.all_gather(observer_places, "obs", axis=1, tiled=True)
    obs_total = every_obs.shape[1]
    obs_blocks = obs_total // OBLK
    kernel = functools.partial(fwh_kernel, amplitude=amplitude, panel_blocks=panel_blocks, window=window, bins_total=bins_total)
    grid_spec = pltpu.PrefetchScalarGridSpec(
        num_scalar_prefetch=1,
        grid=(obs_blocks,),
        in_specs=[
            pl.BlockSpec((OBLK, 3), lambda i, b: (i, 0)),
            pl.BlockSpec((3, local_panels), lambda i, b: (0, 0)),
            pl.BlockSpec((OBLK, local_panels), lambda i, b: (i, 0)),
            pl.BlockSpec((4, local_panels, window), lambda i, b: (0, 0, 0)),
        ],
        out_specs=pl.BlockSpec((None, bins_total, OBLK), lambda i, b: (i // 2, 0, i % 2)),
    )
    totals = pl.pallas_call(
        kernel,
        grid_spec=grid_spec,
        out_shape=jax.ShapeDtypeStruct((obs_blocks // 2, bins_total, 2 * OBLK), jnp.float32),
    )(delay_bins[:, 0, :], every_obs.T, panel_places[0], fraction[:, 0, :], sources[0])
    halves = totals.reshape((2, 2) + totals.shape[1:])
    me = lax.axis_index("obs")
    for bit, dim in ((0, 1), (1, 0)):
        mine = (me >> bit) & 1
        low = lax.index_in_dim(halves, 0, dim, keepdims=False)
        high = lax.index_in_dim(halves, 1, dim, keepdims=False)
        keep = jnp.where(mine == 1, high, low)
        send = jnp.where(mine == 1, low, high)
        pairs = [(p, p ^ (1 << bit)) for p in range(4)]
        halves = keep + lax.ppermute(send, "obs", pairs)
    reduced = halves
    segment_count = segment_owner.shape[0]
    seg_len = bins_total // segment_count
    arranged = reduced.reshape(segment_count, seg_len, reduced.shape[1])
    inverse = jnp.argsort(segment_owner)
    arranged = arranged[inverse]
    rows = -(-seg_len // 8) * 8
    padded = jnp.pad(arranged, ((0, 0), (0, rows - seg_len), (0, 0)))
    return exchange_sum(padded, 8)[:seg_len]


def exchange_kernel(x_ref, out_ref, first, mid, second, sems):
    inner, outer = x_ref.shape[0], x_ref.shape[1]
    me = lax.axis_index("pan")
    my_g = me // inner
    my_z = lax.rem(me, inner)

    def first_copy(zt, zs):
        return pltpu.make_async_remote_copy(
            src_ref=x_ref.at[zt],
            dst_ref=first.at[zs],
            send_sem=sems.at[0, zt],
            recv_sem=sems.at[1, zs],
            device_id={"pan": my_g * inner + zt},
            device_id_type=pl.DeviceIdType.MESH,
        )

    def second_copy(gt, gs):
        return pltpu.make_async_remote_copy(
            src_ref=mid.at[gt],
            dst_ref=second.at[gs],
            send_sem=sems.at[2, gt],
            recv_sem=sems.at[3, gs],
            device_id={"pan": gt * inner + my_z},
            device_id_type=pl.DeviceIdType.MESH,
        )

    def send_first(d, carry):
        first_copy(lax.rem(my_z + d, inner), my_z).start()
        return carry

    lax.fori_loop(1, inner, send_first, 0)

    def take_first(d, total):
        source = lax.rem(my_z + inner - d, inner)
        first_copy(source, source).wait_recv()
        return total + first[source]

    mid[...] = lax.fori_loop(1, inner, take_first, x_ref[my_z])

    def send_second(d, carry):
        second_copy(lax.rem(my_g + d, outer), my_g).start()
        return carry

    lax.fori_loop(1, outer, send_second, 0)

    def take_second(d, total):
        source = lax.rem(my_g + outer - d, outer)
        second_copy(source, source).wait_recv()
        return total + second[source]

    total = lax.fori_loop(1, outer, take_second, mid[my_g])

    def drain_first(d, carry):
        first_copy(lax.rem(my_z + d, inner), my_z).wait_send()
        return carry

    def drain_second(d, carry):
        second_copy(lax.rem(my_g + d, outer), my_g).wait_send()
        return carry

    lax.fori_loop(1, inner, drain_first, 0)
    lax.fori_loop(1, outer, drain_second, 0)
    out_ref[...] = total


def exchange_sum(data, inner):
    count = data.shape[0]
    outer = count // inner
    grouped = data.reshape((outer, inner) + data.shape[1:]).swapaxes(0, 1)
    return pl.pallas_call(
        exchange_kernel,
        out_shape=jax.ShapeDtypeStruct(data.shape[1:], data.dtype),
        in_specs=[pl.BlockSpec(memory_space=pltpu.VMEM)],
        out_specs=pl.BlockSpec(memory_space=pltpu.VMEM),
        scratch_shapes=[
            pltpu.VMEM(grouped.shape, data.dtype),
            pltpu.VMEM((outer,) + data.shape[1:], data.dtype),
            pltpu.VMEM((outer,) + data.shape[1:], data.dtype),
            pltpu.SemaphoreType.DMA((4, max(inner, outer))),
        ],
        compiler_params=pltpu.CompilerParams(has_side_effects=True),
    )(grouped)


def halving_sum(data, axis, bit_order):
    count = data.shape[0]
    levels = count.bit_length() - 1
    me = lax.axis_index(axis)
    data = data.reshape((2,) * levels + data.shape[1:])
    remaining = list(range(levels - 1, -1, -1))
    for bit in bit_order:
        dim = remaining.index(bit)
        mine = (me >> bit) & 1
        low = lax.index_in_dim(data, 0, dim, keepdims=False)
        high = lax.index_in_dim(data, 1, dim, keepdims=False)
        keep = jnp.where(mine == 1, high, low)
        send = jnp.where(mine == 1, low, high)
        pairs = [(p, p ^ (1 << bit)) for p in range(count)]
        data = keep + lax.ppermute(send, axis, pairs)
        remaining.pop(dim)
    return data


def solution(mesh):
    return jax.shard_map(
        per_device,
        mesh=mesh,
        in_specs=(
            P("pan", None, "obs", None),
            P("pan", None, "obs"),
            P(None, "obs"),
            P(None, "pan", "obs"),
            P(None, "pan", "obs"),
            P(),
        ),
        out_specs=P("pan", "obs"),
        check_vma=False,
    )
```

```python
import functools
import math

import jax
import jax.numpy as jnp
from jax import lax
from jax.experimental import pallas as pl
from jax.experimental.pallas import tpu as pltpu
from jax.sharding import PartitionSpec as P

MAXD = 127
OBLK = 128
PBLK = 128


def fwh_kernel(bins_ref, obs_ref, place_ref, frac_ref, src_ref, out_ref, *, amplitude, panel_blocks, window, bins_total):
    ob = pl.program_id(0)
    acc = jnp.zeros((OBLK, bins_total), jnp.float32)
    pad = jnp.zeros((OBLK, bins_total - window), jnp.float32)
    for pb in range(panel_blocks):
        cols = slice(pb * PBLK, (pb + 1) * PBLK)
        seps = [obs_ref[:, c : c + 1] - place_ref[c : c + 1, cols] for c in range(3)]
        dist_sq = seps[0] * seps[0] + seps[1] * seps[1] + seps[2] * seps[2]
        parts = [amplitude / jnp.sqrt(dist_sq)] + [amplitude * sep / dist_sq for sep in seps]
        weight = frac_ref[:, cols].astype(jnp.float32)
        low = None
        high = None
        for c in range(4):
            src = src_ref[c, cols, :]
            lo_w = (parts[c] * (1.0 - weight)).astype(jnp.bfloat16)
            hi_w = (parts[c] * weight).astype(jnp.bfloat16)
            lo_p = jnp.dot(lo_w, src, preferred_element_type=jnp.float32)
            hi_p = jnp.dot(hi_w, src, preferred_element_type=jnp.float32)
            low = lo_p if low is None else low + lo_p
            high = hi_p if high is None else high + hi_p
        shift = bins_ref[ob, pb]
        acc = acc + pltpu.roll(jnp.concatenate([low, pad], axis=1), shift, 1)
        acc = acc + pltpu.roll(jnp.concatenate([high, pad], axis=1), shift + 1, 1)
    out_ref[...] = acc.T


def per_device(sources, panel_places, observer_places, fraction, delay_bins, segment_owner):
    local_panels = sources.shape[2]
    window = sources.shape[3]
    bins_total = window + MAXD + 1
    amplitude = 60.0 / math.sqrt(local_panels * lax.axis_size("obs") * lax.axis_size("pan"))
    panel_blocks = local_panels // PBLK
    every_obs = lax.all_gather(observer_places, "obs", axis=1, tiled=True)
    obs_total = every_obs.shape[1]
    obs_blocks = obs_total // OBLK
    kernel = functools.partial(fwh_kernel, amplitude=amplitude, panel_blocks=panel_blocks, window=window, bins_total=bins_total)
    grid_spec = pltpu.PrefetchScalarGridSpec(
        num_scalar_prefetch=1,
        grid=(obs_blocks,),
        in_specs=[
            pl.BlockSpec((OBLK, 3), lambda i, b: (i, 0)),
            pl.BlockSpec((3, local_panels), lambda i, b: (0, 0)),
            pl.BlockSpec((OBLK, local_panels), lambda i, b: (i, 0)),
            pl.BlockSpec((4, local_panels, window), lambda i, b: (0, 0, 0)),
        ],
        out_specs=pl.BlockSpec((None, bins_total, OBLK), lambda i, b: (i // 2, 0, i % 2)),
    )
    totals = pl.pallas_call(
        kernel,
        grid_spec=grid_spec,
        out_shape=jax.ShapeDtypeStruct((obs_blocks // 2, bins_total, 2 * OBLK), jnp.float32),
    )(delay_bins[:, 0, :], every_obs.T, panel_places[0], fraction[:, 0, :], sources[0])
    halves = totals.reshape((2, 2) + totals.shape[1:])
    me = lax.axis_index("obs")
    for bit, dim in ((0, 1), (1, 0)):
        mine = (me >> bit) & 1
        low = lax.index_in_dim(halves, 0, dim, keepdims=False)
        high = lax.index_in_dim(halves, 1, dim, keepdims=False)
        keep = jnp.where(mine == 1, high, low)
        send = jnp.where(mine == 1, low, high)
        pairs = [(p, p ^ (1 << bit)) for p in range(4)]
        halves = keep + lax.ppermute(send, "obs", pairs)
    reduced = halves
    segment_count = segment_owner.shape[0]
    seg_len = bins_total // segment_count
    arranged = reduced.reshape(segment_count, seg_len, reduced.shape[1])
    inverse = jnp.argsort(segment_owner)
    arranged = arranged[inverse]
    rows = -(-seg_len // 8) * 8
    padded = jnp.pad(arranged, ((0, 0), (0, rows - seg_len), (0, 0)))
    return exchange_sum(padded, 8)[:seg_len]


def exchange_kernel(x_ref, out_ref, first, mid, second, sems):
    inner, outer = x_ref.shape[0], x_ref.shape[1]
    me = lax.axis_index("pan")
    my_g = me // inner
    my_z = lax.rem(me, inner)

    def first_copy(zt, zs):
        return pltpu.make_async_remote_copy(
            src_ref=x_ref.at[zt],
            dst_ref=first.at[zs],
            send_sem=sems.at[0, zt],
            recv_sem=sems.at[1, zs],
            device_id={"pan": my_g * inner + zt},
            device_id_type=pl.DeviceIdType.MESH,
        )

    def second_copy(gt, gs):
        return pltpu.make_async_remote_copy(
            src_ref=mid.at[gt],
            dst_ref=second.at[gs],
            send_sem=sems.at[2, gt],
            recv_sem=sems.at[3, gs],
            device_id={"pan": gt * inner + my_z},
            device_id_type=pl.DeviceIdType.MESH,
        )

    barrier = pltpu.get_barrier_semaphore()

    def knock_first(d, carry):
        pl.semaphore_signal(barrier, inc=1, device_id={"pan": my_g * inner + lax.rem(my_z + d, inner)}, device_id_type=pl.DeviceIdType.MESH)
        return carry

    def knock_second(d, carry):
        pl.semaphore_signal(barrier, inc=1, device_id={"pan": lax.rem(my_g + d, outer) * inner + my_z}, device_id_type=pl.DeviceIdType.MESH)
        return carry

    lax.fori_loop(1, inner, knock_first, 0)
    lax.fori_loop(1, outer, knock_second, 0)
    pl.semaphore_wait(barrier, inner + outer - 2)

    def send_first(d, carry):
        first_copy(lax.rem(my_z + d, inner), my_z).start()
        return carry

    lax.fori_loop(1, inner, send_first, 0)

    def take_first(d, total):
        source = lax.rem(my_z + inner - d, inner)
        first_copy(source, source).wait_recv()
        return total + first[source]

    mid[...] = lax.fori_loop(1, inner, take_first, x_ref[my_z])

    def send_second(d, carry):
        second_copy(lax.rem(my_g + d, outer), my_g).start()
        return carry

    lax.fori_loop(1, outer, send_second, 0)

    def take_second(d, total):
        source = lax.rem(my_g + outer - d, outer)
        second_copy(source, source).wait_recv()
        return total + second[source]

    total = lax.fori_loop(1, outer, take_second, mid[my_g])

    def drain_first(d, carry):
        first_copy(lax.rem(my_z + d, inner), my_z).wait_send()
        return carry

    def drain_second(d, carry):
        second_copy(lax.rem(my_g + d, outer), my_g).wait_send()
        return carry

    lax.fori_loop(1, inner, drain_first, 0)
    lax.fori_loop(1, outer, drain_second, 0)
    out_ref[...] = total


def exchange_sum(data, inner):
    count = data.shape[0]
    outer = count // inner
    grouped = data.reshape((outer, inner) + data.shape[1:]).swapaxes(0, 1)
    return pl.pallas_call(
        exchange_kernel,
        out_shape=jax.ShapeDtypeStruct(data.shape[1:], data.dtype),
        in_specs=[pl.BlockSpec(memory_space=pltpu.VMEM)],
        out_specs=pl.BlockSpec(memory_space=pltpu.VMEM),
        scratch_shapes=[
            pltpu.VMEM(grouped.shape, data.dtype),
            pltpu.VMEM((outer,) + data.shape[1:], data.dtype),
            pltpu.VMEM((outer,) + data.shape[1:], data.dtype),
            pltpu.SemaphoreType.DMA((4, max(inner, outer))),
        ],
        compiler_params=pltpu.CompilerParams(collective_id=0, has_side_effects=True),
    )(grouped)


def halving_sum(data, axis, bit_order):
    count = data.shape[0]
    levels = count.bit_length() - 1
    me = lax.axis_index(axis)
    data = data.reshape((2,) * levels + data.shape[1:])
    remaining = list(range(levels - 1, -1, -1))
    for bit in bit_order:
        dim = remaining.index(bit)
        mine = (me >> bit) & 1
        low = lax.index_in_dim(data, 0, dim, keepdims=False)
        high = lax.index_in_dim(data, 1, dim, keepdims=False)
        keep = jnp.where(mine == 1, high, low)
        send = jnp.where(mine == 1, low, high)
        pairs = [(p, p ^ (1 << bit)) for p in range(count)]
        data = keep + lax.ppermute(send, axis, pairs)
        remaining.pop(dim)
    return data


def solution(mesh):
    return jax.shard_map(
        per_device,
        mesh=mesh,
        in_specs=(
            P("pan", None, "obs", None),
            P("pan", None, "obs"),
            P(None, "obs"),
            P(None, "pan", "obs"),
            P(None, "pan", "obs"),
            P(),
        ),
        out_specs=P("pan", "obs"),
        check_vma=False,
    )
```

```python
import functools
import math

import jax
import jax.numpy as jnp
from jax import lax
from jax.experimental import pallas as pl
from jax.experimental.pallas import tpu as pltpu
from jax.sharding import PartitionSpec as P

MAXD = 127
OBLK = 128
PBLK = 128


def fwh_kernel(bins_ref, obs_ref, place_ref, frac_ref, src_ref, out_ref, *, amplitude, panel_blocks, window, bins_total):
    ob = pl.program_id(0)
    acc = jnp.zeros((OBLK, bins_total), jnp.float32)
    pad = jnp.zeros((OBLK, bins_total - window), jnp.float32)
    for pb in range(panel_blocks):
        cols = slice(pb * PBLK, (pb + 1) * PBLK)
        seps = [obs_ref[:, c : c + 1] - place_ref[c : c + 1, cols] for c in range(3)]
        dist_sq = seps[0] * seps[0] + seps[1] * seps[1] + seps[2] * seps[2]
        parts = [amplitude / jnp.sqrt(dist_sq)] + [amplitude * sep / dist_sq for sep in seps]
        weight = frac_ref[:, cols].astype(jnp.float32)
        low = None
        high = None
        for c in range(4):
            src = src_ref[c, cols, :]
            lo_w = (parts[c] * (1.0 - weight)).astype(jnp.bfloat16)
            hi_w = (parts[c] * weight).astype(jnp.bfloat16)
            lo_p = jnp.dot(lo_w, src, preferred_element_type=jnp.float32)
            hi_p = jnp.dot(hi_w, src, preferred_element_type=jnp.float32)
            low = lo_p if low is None else low + lo_p
            high = hi_p if high is None else high + hi_p
        shift = bins_ref[ob, pb]
        acc = acc + pltpu.roll(jnp.concatenate([low, pad], axis=1), shift, 1)
        acc = acc + pltpu.roll(jnp.concatenate([high, pad], axis=1), shift + 1, 1)
    out_ref[...] = acc.T


def per_device(sources, panel_places, observer_places, fraction, delay_bins, segment_owner):
    local_panels = sources.shape[2]
    window = sources.shape[3]
    bins_total = window + MAXD + 1
    amplitude = 60.0 / math.sqrt(local_panels * lax.axis_size("obs") * lax.axis_size("pan"))
    panel_blocks = local_panels // PBLK
    every_obs = lax.all_gather(observer_places, "obs", axis=1, tiled=True)
    obs_total = every_obs.shape[1]
    obs_blocks = obs_total // OBLK
    kernel = functools.partial(fwh_kernel, amplitude=amplitude, panel_blocks=panel_blocks, window=window, bins_total=bins_total)
    grid_spec = pltpu.PrefetchScalarGridSpec(
        num_scalar_prefetch=1,
        grid=(obs_blocks,),
        in_specs=[
            pl.BlockSpec((OBLK, 3), lambda i, b: (i, 0)),
            pl.BlockSpec((3, local_panels), lambda i, b: (0, 0)),
            pl.BlockSpec((OBLK, local_panels), lambda i, b: (i, 0)),
            pl.BlockSpec((4, local_panels, window), lambda i, b: (0, 0, 0)),
        ],
        out_specs=pl.BlockSpec((None, bins_total, OBLK), lambda i, b: (i // 2, 0, i % 2)),
    )
    totals = pl.pallas_call(
        kernel,
        grid_spec=grid_spec,
        out_shape=jax.ShapeDtypeStruct((obs_blocks // 2, bins_total, 2 * OBLK), jnp.float32),
    )(delay_bins[:, 0, :], every_obs.T, panel_places[0], fraction[:, 0, :], sources[0])
    halves = totals.reshape((2, 2) + totals.shape[1:])
    me = lax.axis_index("obs")
    for bit, dim in ((0, 1), (1, 0)):
        mine = (me >> bit) & 1
        low = lax.index_in_dim(halves, 0, dim, keepdims=False)
        high = lax.index_in_dim(halves, 1, dim, keepdims=False)
        keep = jnp.where(mine == 1, high, low)
        send = jnp.where(mine == 1, low, high)
        pairs = [(p, p ^ (1 << bit)) for p in range(4)]
        halves = keep + lax.ppermute(send, "obs", pairs)
    reduced = halves
    segment_count = segment_owner.shape[0]
    seg_len = bins_total // segment_count
    arranged = reduced.reshape(segment_count, seg_len, reduced.shape[1])
    inverse = jnp.argsort(segment_owner)
    arranged = arranged[inverse]
    rows = -(-seg_len // 8) * 8
    padded = jnp.pad(arranged, ((0, 0), (0, rows - seg_len), (0, 0)))
    return exchange_sum(padded)[:seg_len]


def exchange_kernel(x_ref, out_ref, slots, send_sem, recv_sem):
    count = x_ref.shape[0]
    me = lax.axis_index("pan")

    def send(d, carry):
        target = lax.rem(me + d, count)
        pltpu.make_async_remote_copy(
            src_ref=x_ref.at[target],
            dst_ref=slots.at[me],
            send_sem=send_sem.at[target],
            recv_sem=recv_sem.at[me],
            device_id={"pan": target},
            device_id_type=pl.DeviceIdType.MESH,
        ).start()
        return carry

    barrier = pltpu.get_barrier_semaphore()

    def knock(d, carry):
        pl.semaphore_signal(barrier, inc=1, device_id={"pan": lax.rem(me + d, count)}, device_id_type=pl.DeviceIdType.MESH)
        return carry

    lax.fori_loop(1, count, knock, 0)
    pl.semaphore_wait(barrier, count - 1)
    lax.fori_loop(1, count, send, 0)
    total = x_ref[me]

    def gather(d, total):
        source = lax.rem(me + count - d, count)
        pltpu.make_async_remote_copy(
            src_ref=x_ref.at[source],
            dst_ref=slots.at[source],
            send_sem=send_sem.at[source],
            recv_sem=recv_sem.at[source],
            device_id={"pan": source},
            device_id_type=pl.DeviceIdType.MESH,
        ).wait_recv()
        return total + slots[source]

    total = lax.fori_loop(1, count, gather, total)

    def drain(d, carry):
        target = lax.rem(me + d, count)
        pltpu.make_async_remote_copy(
            src_ref=x_ref.at[target],
            dst_ref=slots.at[me],
            send_sem=send_sem.at[target],
            recv_sem=recv_sem.at[me],
            device_id={"pan": target},
            device_id_type=pl.DeviceIdType.MESH,
        ).wait_send()
        return carry

    lax.fori_loop(1, count, drain, 0)
    out_ref[...] = total


def exchange_sum(data):
    count = data.shape[0]
    return pl.pallas_call(
        exchange_kernel,
        out_shape=jax.ShapeDtypeStruct(data.shape[1:], data.dtype),
        in_specs=[pl.BlockSpec(memory_space=pltpu.VMEM)],
        out_specs=pl.BlockSpec(memory_space=pltpu.VMEM),
        scratch_shapes=[
            pltpu.VMEM(data.shape, data.dtype),
            pltpu.SemaphoreType.DMA((count,)),
            pltpu.SemaphoreType.DMA((count,)),
        ],
        compiler_params=pltpu.CompilerParams(collective_id=0, has_side_effects=True),
    )(data)


def halving_sum(data, axis, bit_order):
    count = data.shape[0]
    levels = count.bit_length() - 1
    me = lax.axis_index(axis)
    data = data.reshape((2,) * levels + data.shape[1:])
    remaining = list(range(levels - 1, -1, -1))
    for bit in bit_order:
        dim = remaining.index(bit)
        mine = (me >> bit) & 1
        low = lax.index_in_dim(data, 0, dim, keepdims=False)
        high = lax.index_in_dim(data, 1, dim, keepdims=False)
        keep = jnp.where(mine == 1, high, low)
        send = jnp.where(mine == 1, low, high)
        pairs = [(p, p ^ (1 << bit)) for p in range(count)]
        data = keep + lax.ppermute(send, axis, pairs)
        remaining.pop(dim)
    return data


def solution(mesh):
    return jax.shard_map(
        per_device,
        mesh=mesh,
        in_specs=(
            P("pan", None, "obs", None),
            P("pan", None, "obs"),
            P(None, "obs"),
            P(None, "pan", "obs"),
            P(None, "pan", "obs"),
            P(),
        ),
        out_specs=P("pan", "obs"),
        check_vma=False,
    )
```

```python
import functools
import math

import jax
import jax.numpy as jnp
from jax import lax
from jax.experimental import pallas as pl
from jax.experimental.pallas import tpu as pltpu
from jax.sharding import PartitionSpec as P

MAXD = 127
OBLK = 128
PBLK = 128


def fwh_kernel(bins_ref, obs_ref, place_ref, frac_ref, src_ref, out_ref, *, amplitude, panel_blocks, window, bins_total):
    ob = pl.program_id(0)
    here = obs_ref[...].T
    acc = jnp.zeros((OBLK, bins_total), jnp.float32)
    pad = jnp.zeros((OBLK, bins_total - window), jnp.float32)
    for pb in range(panel_blocks):
        cols = slice(pb * PBLK, (pb + 1) * PBLK)
        seps = [here[:, c : c + 1] - place_ref[c : c + 1, cols] for c in range(3)]
        dist_sq = seps[0] * seps[0] + seps[1] * seps[1] + seps[2] * seps[2]
        parts = [amplitude / jnp.sqrt(dist_sq)] + [amplitude * sep / dist_sq for sep in seps]
        weight = frac_ref[:, cols].astype(jnp.float32)
        low = None
        high = None
        for c in range(4):
            src = src_ref[c, cols, :]
            lo_w = (parts[c] * (1.0 - weight)).astype(jnp.bfloat16)
            hi_w = (parts[c] * weight).astype(jnp.bfloat16)
            lo_p = jnp.dot(lo_w, src, preferred_element_type=jnp.float32)
            hi_p = jnp.dot(hi_w, src, preferred_element_type=jnp.float32)
            low = lo_p if low is None else low + lo_p
            high = hi_p if high is None else high + hi_p
        shift = bins_ref[ob, 0, pb]
        acc = acc + pltpu.roll(jnp.concatenate([low, pad], axis=1), shift, 1)
        acc = acc + pltpu.roll(jnp.concatenate([high, pad], axis=1), shift + 1, 1)
    out_ref[...] = acc.T


def per_device(sources, panel_places, observer_places, fraction, delay_bins, segment_owner):
    local_panels = sources.shape[2]
    window = sources.shape[3]
    bins_total = window + MAXD + 1
    amplitude = 60.0 / math.sqrt(local_panels * lax.axis_size("obs") * lax.axis_size("pan"))
    panel_blocks = local_panels // PBLK
    every_obs = lax.all_gather(observer_places, "obs", axis=1, tiled=True)
    obs_total = every_obs.shape[1]
    obs_blocks = obs_total // OBLK
    kernel = functools.partial(fwh_kernel, amplitude=amplitude, panel_blocks=panel_blocks, window=window, bins_total=bins_total)
    grid_spec = pltpu.PrefetchScalarGridSpec(
        num_scalar_prefetch=1,
        grid=(obs_blocks,),
        in_specs=[
            pl.BlockSpec((3, OBLK), lambda i, b: (0, i)),
            pl.BlockSpec((3, local_panels), lambda i, b: (0, 0)),
            pl.BlockSpec((OBLK, local_panels), lambda i, b: (i, 0)),
            pl.BlockSpec((4, local_panels, window), lambda i, b: (0, 0, 0)),
        ],
        out_specs=pl.BlockSpec((None, bins_total, OBLK), lambda i, b: (i // 2, 0, i % 2)),
    )
    totals = pl.pallas_call(
        kernel,
        grid_spec=grid_spec,
        out_shape=jax.ShapeDtypeStruct((obs_blocks // 2, bins_total, 2 * OBLK), jnp.float32),
    )(delay_bins, every_obs, panel_places[0], fraction[:, 0, :], sources[0])
    halves = totals.reshape((2, 2) + totals.shape[1:])
    me = lax.axis_index("obs")
    for bit, dim in ((0, 1), (1, 0)):
        mine = (me >> bit) & 1
        low = lax.index_in_dim(halves, 0, dim, keepdims=False)
        high = lax.index_in_dim(halves, 1, dim, keepdims=False)
        keep = jnp.where(mine == 1, high, low)
        send = jnp.where(mine == 1, low, high)
        pairs = [(p, p ^ (1 << bit)) for p in range(4)]
        halves = keep + lax.ppermute(send, "obs", pairs)
    reduced = halves
    segment_count = segment_owner.shape[0]
    seg_len = bins_total // segment_count
    arranged = reduced.reshape(segment_count, seg_len, reduced.shape[1])
    inverse = jnp.argsort(segment_owner)
    arranged = arranged[inverse]
    rows = -(-seg_len // 8) * 8
    padded = jnp.pad(arranged, ((0, 0), (0, rows - seg_len), (0, 0)))
    return exchange_sum(padded)[:seg_len]


def exchange_kernel(x_ref, out_ref, slots, send_sem, recv_sem):
    count = x_ref.shape[0]
    me = lax.axis_index("pan")

    def send(d, carry):
        target = lax.rem(me + d, count)
        pltpu.make_async_remote_copy(
            src_ref=x_ref.at[target],
            dst_ref=slots.at[me],
            send_sem=send_sem.at[target],
            recv_sem=recv_sem.at[me],
            device_id={"pan": target},
            device_id_type=pl.DeviceIdType.MESH,
        ).start()
        return carry

    barrier = pltpu.get_barrier_semaphore()

    def knock(d, carry):
        pl.semaphore_signal(barrier, inc=1, device_id={"pan": lax.rem(me + d, count)}, device_id_type=pl.DeviceIdType.MESH)
        return carry

    lax.fori_loop(1, count, knock, 0)
    pl.semaphore_wait(barrier, count - 1)
    lax.fori_loop(1, count, send, 0)
    total = x_ref[me]

    def gather(d, total):
        source = lax.rem(me + count - d, count)
        pltpu.make_async_remote_copy(
            src_ref=x_ref.at[source],
            dst_ref=slots.at[source],
            send_sem=send_sem.at[source],
            recv_sem=recv_sem.at[source],
            device_id={"pan": source},
            device_id_type=pl.DeviceIdType.MESH,
        ).wait_recv()
        return total + slots[source]

    total = lax.fori_loop(1, count, gather, total)

    def drain(d, carry):
        target = lax.rem(me + d, count)
        pltpu.make_async_remote_copy(
            src_ref=x_ref.at[target],
            dst_ref=slots.at[me],
            send_sem=send_sem.at[target],
            recv_sem=recv_sem.at[me],
            device_id={"pan": target},
            device_id_type=pl.DeviceIdType.MESH,
        ).wait_send()
        return carry

    lax.fori_loop(1, count, drain, 0)
    out_ref[...] = total


def exchange_sum(data):
    count = data.shape[0]
    return pl.pallas_call(
        exchange_kernel,
        out_shape=jax.ShapeDtypeStruct(data.shape[1:], data.dtype),
        in_specs=[pl.BlockSpec(memory_space=pltpu.VMEM)],
        out_specs=pl.BlockSpec(memory_space=pltpu.VMEM),
        scratch_shapes=[
            pltpu.VMEM(data.shape, data.dtype),
            pltpu.SemaphoreType.DMA((count,)),
            pltpu.SemaphoreType.DMA((count,)),
        ],
        compiler_params=pltpu.CompilerParams(collective_id=0, has_side_effects=True),
    )(data)


def halving_sum(data, axis, bit_order):
    count = data.shape[0]
    levels = count.bit_length() - 1
    me = lax.axis_index(axis)
    data = data.reshape((2,) * levels + data.shape[1:])
    remaining = list(range(levels - 1, -1, -1))
    for bit in bit_order:
        dim = remaining.index(bit)
        mine = (me >> bit) & 1
        low = lax.index_in_dim(data, 0, dim, keepdims=False)
        high = lax.index_in_dim(data, 1, dim, keepdims=False)
        keep = jnp.where(mine == 1, high, low)
        send = jnp.where(mine == 1, low, high)
        pairs = [(p, p ^ (1 << bit)) for p in range(count)]
        data = keep + lax.ppermute(send, axis, pairs)
        remaining.pop(dim)
    return data


def solution(mesh):
    return jax.shard_map(
        per_device,
        mesh=mesh,
        in_specs=(
            P("pan", None, "obs", None),
            P("pan", None, "obs"),
            P(None, "obs"),
            P(None, "pan", "obs"),
            P(None, "pan", "obs"),
            P(),
        ),
        out_specs=P("pan", "obs"),
        check_vma=False,
    )
```

```python
import functools
import math

import jax
import jax.numpy as jnp
from jax import lax
from jax.experimental import pallas as pl
from jax.experimental.pallas import tpu as pltpu
from jax.sharding import PartitionSpec as P

MAXD = 127
OBLK = 128
PBLK = 128


def fwh_kernel(bins_ref, obs_ref, place_ref, frac_ref, src_ref, out_ref, *, amplitude, panel_blocks, window, bins_total):
    ob = pl.program_id(0)
    here = obs_ref[...].T
    acc = jnp.zeros((OBLK, bins_total), jnp.float32)
    pad = jnp.zeros((OBLK, bins_total - window), jnp.float32)
    for pb in range(panel_blocks):
        cols = slice(pb * PBLK, (pb + 1) * PBLK)
        seps = [here[:, c : c + 1] - place_ref[c : c + 1, cols] for c in range(3)]
        dist_sq = seps[0] * seps[0] + seps[1] * seps[1] + seps[2] * seps[2]
        parts = [amplitude / jnp.sqrt(dist_sq)] + [amplitude * sep / dist_sq for sep in seps]
        weight = frac_ref[:, cols].astype(jnp.float32)
        low = None
        high = None
        for c in range(4):
            src = src_ref[c, cols, :]
            lo_w = (parts[c] * (1.0 - weight)).astype(jnp.bfloat16)
            hi_w = (parts[c] * weight).astype(jnp.bfloat16)
            lo_p = jnp.dot(lo_w, src, preferred_element_type=jnp.float32)
            hi_p = jnp.dot(hi_w, src, preferred_element_type=jnp.float32)
            low = lo_p if low is None else low + lo_p
            high = hi_p if high is None else high + hi_p
        shift = bins_ref[ob, 0, pb]
        acc = acc + pltpu.roll(jnp.concatenate([low, pad], axis=1), shift, 1)
        acc = acc + pltpu.roll(jnp.concatenate([high, pad], axis=1), shift + 1, 1)
    out_ref[...] = acc.T


def per_device(sources, panel_places, observer_places, fraction, delay_bins, segment_owner):
    local_panels = sources.shape[2]
    window = sources.shape[3]
    bins_total = window + MAXD + 1
    amplitude = 60.0 / math.sqrt(local_panels * lax.axis_size("obs") * lax.axis_size("pan"))
    panel_blocks = local_panels // PBLK
    obs_count = lax.axis_size("obs")
    obs_me = lax.axis_index("obs")
    arrived = [observer_places] + [
        lax.ppermute(observer_places, "obs", [(p, p ^ k) for p in range(obs_count)]) for k in range(1, obs_count)
    ]
    blocks = []
    for q in range(obs_count):
        block = arrived[0]
        for k in range(1, obs_count):
            block = jnp.where((obs_me ^ k) == q, arrived[k], block)
        blocks.append(block)
    every_obs = jnp.concatenate(blocks, axis=1)
    obs_total = every_obs.shape[1]
    obs_blocks = obs_total // OBLK
    kernel = functools.partial(fwh_kernel, amplitude=amplitude, panel_blocks=panel_blocks, window=window, bins_total=bins_total)
    grid_spec = pltpu.PrefetchScalarGridSpec(
        num_scalar_prefetch=1,
        grid=(obs_blocks,),
        in_specs=[
            pl.BlockSpec((3, OBLK), lambda i, b: (0, i)),
            pl.BlockSpec((3, local_panels), lambda i, b: (0, 0)),
            pl.BlockSpec((OBLK, local_panels), lambda i, b: (i, 0)),
            pl.BlockSpec((4, local_panels, window), lambda i, b: (0, 0, 0)),
        ],
        out_specs=pl.BlockSpec((None, bins_total, OBLK), lambda i, b: (i // 2, 0, i % 2)),
    )
    totals = pl.pallas_call(
        kernel,
        grid_spec=grid_spec,
        out_shape=jax.ShapeDtypeStruct((obs_blocks // 2, bins_total, 2 * OBLK), jnp.float32),
    )(delay_bins, every_obs, panel_places[0], fraction[:, 0, :], sources[0])
    halves = totals.reshape((2, 2) + totals.shape[1:])
    me = lax.axis_index("obs")
    for bit, dim in ((0, 1), (1, 0)):
        mine = (me >> bit) & 1
        low = lax.index_in_dim(halves, 0, dim, keepdims=False)
        high = lax.index_in_dim(halves, 1, dim, keepdims=False)
        keep = jnp.where(mine == 1, high, low)
        send = jnp.where(mine == 1, low, high)
        pairs = [(p, p ^ (1 << bit)) for p in range(4)]
        halves = keep + lax.ppermute(send, "obs", pairs)
    reduced = halves
    segment_count = segment_owner.shape[0]
    seg_len = bins_total // segment_count
    arranged = reduced.reshape(segment_count, seg_len, reduced.shape[1])
    inverse = jnp.argsort(segment_owner)
    arranged = arranged[inverse]
    rows = -(-seg_len // 8) * 8
    padded = jnp.pad(arranged, ((0, 0), (0, rows - seg_len), (0, 0)))
    return exchange_sum(padded)[:seg_len]


def exchange_kernel(x_ref, out_ref, slots, send_sem, recv_sem):
    count = x_ref.shape[0]
    me = lax.axis_index("pan")

    def send(d, carry):
        target = lax.rem(me + d, count)
        pltpu.make_async_remote_copy(
            src_ref=x_ref.at[target],
            dst_ref=slots.at[me],
            send_sem=send_sem.at[target],
            recv_sem=recv_sem.at[me],
            device_id={"pan": target},
            device_id_type=pl.DeviceIdType.MESH,
        ).start()
        return carry

    barrier = pltpu.get_barrier_semaphore()

    def knock(d, carry):
        pl.semaphore_signal(barrier, inc=1, device_id={"pan": lax.rem(me + d, count)}, device_id_type=pl.DeviceIdType.MESH)
        return carry

    lax.fori_loop(1, count, knock, 0)
    pl.semaphore_wait(barrier, count - 1)
    lax.fori_loop(1, count, send, 0)
    total = x_ref[me]

    def gather(d, total):
        source = lax.rem(me + count - d, count)
        pltpu.make_async_remote_copy(
            src_ref=x_ref.at[source],
            dst_ref=slots.at[source],
            send_sem=send_sem.at[source],
            recv_sem=recv_sem.at[source],
            device_id={"pan": source},
            device_id_type=pl.DeviceIdType.MESH,
        ).wait_recv()
        return total + slots[source]

    total = lax.fori_loop(1, count, gather, total)

    def drain(d, carry):
        target = lax.rem(me + d, count)
        pltpu.make_async_remote_copy(
            src_ref=x_ref.at[target],
            dst_ref=slots.at[me],
            send_sem=send_sem.at[target],
            recv_sem=recv_sem.at[me],
            device_id={"pan": target},
            device_id_type=pl.DeviceIdType.MESH,
        ).wait_send()
        return carry

    lax.fori_loop(1, count, drain, 0)
    out_ref[...] = total


def exchange_sum(data):
    count = data.shape[0]
    return pl.pallas_call(
        exchange_kernel,
        out_shape=jax.ShapeDtypeStruct(data.shape[1:], data.dtype),
        in_specs=[pl.BlockSpec(memory_space=pltpu.VMEM)],
        out_specs=pl.BlockSpec(memory_space=pltpu.VMEM),
        scratch_shapes=[
            pltpu.VMEM(data.shape, data.dtype),
            pltpu.SemaphoreType.DMA((count,)),
            pltpu.SemaphoreType.DMA((count,)),
        ],
        compiler_params=pltpu.CompilerParams(collective_id=0, has_side_effects=True),
    )(data)


def halving_sum(data, axis, bit_order):
    count = data.shape[0]
    levels = count.bit_length() - 1
    me = lax.axis_index(axis)
    data = data.reshape((2,) * levels + data.shape[1:])
    remaining = list(range(levels - 1, -1, -1))
    for bit in bit_order:
        dim = remaining.index(bit)
        mine = (me >> bit) & 1
        low = lax.index_in_dim(data, 0, dim, keepdims=False)
        high = lax.index_in_dim(data, 1, dim, keepdims=False)
        keep = jnp.where(mine == 1, high, low)
        send = jnp.where(mine == 1, low, high)
        pairs = [(p, p ^ (1 << bit)) for p in range(count)]
        data = keep + lax.ppermute(send, axis, pairs)
        remaining.pop(dim)
    return data


def solution(mesh):
    return jax.shard_map(
        per_device,
        mesh=mesh,
        in_specs=(
            P("pan", None, "obs", None),
            P("pan", None, "obs"),
            P(None, "obs"),
            P(None, "pan", "obs"),
            P(None, "pan", "obs"),
            P(),
        ),
        out_specs=P("pan", "obs"),
        check_vma=False,
    )
```

```python
import functools
import math

import jax
import jax.numpy as jnp
from jax import lax
from jax.experimental import pallas as pl
from jax.experimental.pallas import tpu as pltpu
from jax.sharding import PartitionSpec as P

MAXD = 127
OBLK = 128
PBLK = 128


def fwh_kernel(bins_ref, order_ref, obs_ref, place_ref, frac_ref, src_ref, out_ref, *, amplitude, panel_blocks, window, bins_total):
    ob = order_ref[pl.program_id(0)]
    here = obs_ref[...].T
    acc = jnp.zeros((OBLK, bins_total), jnp.float32)
    pad = jnp.zeros((OBLK, bins_total - window), jnp.float32)
    for pb in range(panel_blocks):
        cols = slice(pb * PBLK, (pb + 1) * PBLK)
        seps = [here[:, c : c + 1] - place_ref[c : c + 1, cols] for c in range(3)]
        dist_sq = seps[0] * seps[0] + seps[1] * seps[1] + seps[2] * seps[2]
        parts = [amplitude / jnp.sqrt(dist_sq)] + [amplitude * sep / dist_sq for sep in seps]
        weight = frac_ref[:, cols].astype(jnp.float32)
        low = None
        high = None
        for c in range(4):
            src = src_ref[c, cols, :]
            lo_w = (parts[c] * (1.0 - weight)).astype(jnp.bfloat16)
            hi_w = (parts[c] * weight).astype(jnp.bfloat16)
            lo_p = jnp.dot(lo_w, src, preferred_element_type=jnp.float32)
            hi_p = jnp.dot(hi_w, src, preferred_element_type=jnp.float32)
            low = lo_p if low is None else low + lo_p
            high = hi_p if high is None else high + hi_p
        shift = bins_ref[ob, 0, pb]
        acc = acc + pltpu.roll(jnp.concatenate([low, pad], axis=1), shift, 1)
        acc = acc + pltpu.roll(jnp.concatenate([high, pad], axis=1), shift + 1, 1)
    out_ref[...] = acc.T


def per_device(sources, panel_places, observer_places, fraction, delay_bins, segment_owner):
    local_panels = sources.shape[2]
    window = sources.shape[3]
    bins_total = window + MAXD + 1
    amplitude = 60.0 / math.sqrt(local_panels * lax.axis_size("obs") * lax.axis_size("pan"))
    panel_blocks = local_panels // PBLK
    obs_count = lax.axis_size("obs")
    obs_me = lax.axis_index("obs")
    arrived = [observer_places] + [
        lax.ppermute(observer_places, "obs", [(p, p ^ k) for p in range(obs_count)]) for k in range(1, obs_count)
    ]
    blocks = []
    for q in range(obs_count):
        block = arrived[0]
        for k in range(1, obs_count):
            block = jnp.where((obs_me ^ k) == q, arrived[k], block)
        blocks.append(block)
    every_obs = jnp.concatenate(blocks, axis=1)
    obs_total = every_obs.shape[1]
    obs_blocks = obs_total // OBLK
    kernel = functools.partial(fwh_kernel, amplitude=amplitude, panel_blocks=panel_blocks, window=window, bins_total=bins_total)

    def blocks_of(order):
        grid_spec = pltpu.PrefetchScalarGridSpec(
            num_scalar_prefetch=2,
            grid=(order.shape[0],),
            in_specs=[
                pl.BlockSpec((3, OBLK), lambda i, b, o: (0, o[i])),
                pl.BlockSpec((3, local_panels), lambda i, b, o: (0, 0)),
                pl.BlockSpec((OBLK, local_panels), lambda i, b, o: (o[i], 0)),
                pl.BlockSpec((4, local_panels, window), lambda i, b, o: (0, 0, 0)),
            ],
            out_specs=pl.BlockSpec((None, bins_total, OBLK), lambda i, b, o: (i, 0, 0)),
        )
        return pl.pallas_call(
            kernel,
            grid_spec=grid_spec,
            out_shape=jax.ShapeDtypeStruct((order.shape[0], bins_total, OBLK), jnp.float32),
        )(delay_bins, order, every_obs, panel_places[0], fraction[:, 0, :], sources[0])

    low_bit = obs_me & 1
    high_bit = obs_me >> 1
    pair = jnp.arange(2, dtype=jnp.int32)

    def group_blocks(high, low):
        return 2 * (2 * high + low) + pair

    first = blocks_of(jnp.concatenate([group_blocks(0, 1 - low_bit), group_blocks(1, 1 - low_bit)]))
    first_in = lax.ppermute(first, "obs", [(p, p ^ 1) for p in range(obs_count)])
    second = blocks_of(group_blocks(1 - high_bit, low_bit))
    second = second + jnp.where(high_bit == 1, first_in[:2], first_in[2:])
    second_in = lax.ppermute(second, "obs", [(p, p ^ 2) for p in range(obs_count)])
    own = blocks_of(group_blocks(high_bit, low_bit))
    own = own + jnp.where(high_bit == 1, first_in[2:], first_in[:2]) + second_in
    halves = jnp.concatenate([own[0], own[1]], axis=1)
    reduced = halves
    segment_count = segment_owner.shape[0]
    seg_len = bins_total // segment_count
    arranged = reduced.reshape(segment_count, seg_len, reduced.shape[1])
    inverse = jnp.argsort(segment_owner)
    arranged = arranged[inverse]
    rows = -(-seg_len // 8) * 8
    padded = jnp.pad(arranged, ((0, 0), (0, rows - seg_len), (0, 0)))
    return exchange_sum(padded)[:seg_len]


def exchange_kernel(x_ref, out_ref, slots, send_sem, recv_sem):
    count = x_ref.shape[0]
    me = lax.axis_index("pan")

    def send(d, carry):
        target = lax.rem(me + d, count)
        pltpu.make_async_remote_copy(
            src_ref=x_ref.at[target],
            dst_ref=slots.at[me],
            send_sem=send_sem.at[target],
            recv_sem=recv_sem.at[me],
            device_id={"pan": target},
            device_id_type=pl.DeviceIdType.MESH,
        ).start()
        return carry

    barrier = pltpu.get_barrier_semaphore()

    def knock(d, carry):
        pl.semaphore_signal(barrier, inc=1, device_id={"pan": lax.rem(me + d, count)}, device_id_type=pl.DeviceIdType.MESH)
        return carry

    lax.fori_loop(1, count, knock, 0)
    pl.semaphore_wait(barrier, count - 1)
    lax.fori_loop(1, count, send, 0)
    total = x_ref[me]

    def gather(d, total):
        source = lax.rem(me + count - d, count)
        pltpu.make_async_remote_copy(
            src_ref=x_ref.at[source],
            dst_ref=slots.at[source],
            send_sem=send_sem.at[source],
            recv_sem=recv_sem.at[source],
            device_id={"pan": source},
            device_id_type=pl.DeviceIdType.MESH,
        ).wait_recv()
        return total + slots[source]

    total = lax.fori_loop(1, count, gather, total)

    def drain(d, carry):
        target = lax.rem(me + d, count)
        pltpu.make_async_remote_copy(
            src_ref=x_ref.at[target],
            dst_ref=slots.at[me],
            send_sem=send_sem.at[target],
            recv_sem=recv_sem.at[me],
            device_id={"pan": target},
            device_id_type=pl.DeviceIdType.MESH,
        ).wait_send()
        return carry

    lax.fori_loop(1, count, drain, 0)
    out_ref[...] = total


def exchange_sum(data):
    count = data.shape[0]
    return pl.pallas_call(
        exchange_kernel,
        out_shape=jax.ShapeDtypeStruct(data.shape[1:], data.dtype),
        in_specs=[pl.BlockSpec(memory_space=pltpu.VMEM)],
        out_specs=pl.BlockSpec(memory_space=pltpu.VMEM),
        scratch_shapes=[
            pltpu.VMEM(data.shape, data.dtype),
            pltpu.SemaphoreType.DMA((count,)),
            pltpu.SemaphoreType.DMA((count,)),
        ],
        compiler_params=pltpu.CompilerParams(collective_id=0, has_side_effects=True),
    )(data)


def halving_sum(data, axis, bit_order):
    count = data.shape[0]
    levels = count.bit_length() - 1
    me = lax.axis_index(axis)
    data = data.reshape((2,) * levels + data.shape[1:])
    remaining = list(range(levels - 1, -1, -1))
    for bit in bit_order:
        dim = remaining.index(bit)
        mine = (me >> bit) & 1
        low = lax.index_in_dim(data, 0, dim, keepdims=False)
        high = lax.index_in_dim(data, 1, dim, keepdims=False)
        keep = jnp.where(mine == 1, high, low)
        send = jnp.where(mine == 1, low, high)
        pairs = [(p, p ^ (1 << bit)) for p in range(count)]
        data = keep + lax.ppermute(send, axis, pairs)
        remaining.pop(dim)
    return data


def solution(mesh):
    return jax.shard_map(
        per_device,
        mesh=mesh,
        in_specs=(
            P("pan", None, "obs", None),
            P("pan", None, "obs"),
            P(None, "obs"),
            P(None, "pan", "obs"),
            P(None, "pan", "obs"),
            P(),
        ),
        out_specs=P("pan", "obs"),
        check_vma=False,
    )
```

```python
import functools
import math

import jax
import jax.numpy as jnp
from jax import lax
from jax.experimental import pallas as pl
from jax.experimental.pallas import tpu as pltpu
from jax.sharding import PartitionSpec as P

MAXD = 127
OBLK = 128
PBLK = 128


def fwh_kernel(bins_ref, obs_ref, place_ref, frac_ref, src_ref, out_ref, *, amplitude, panel_blocks, window, bins_total):
    ob = pl.program_id(0)
    here = obs_ref[...].T
    acc = jnp.zeros((OBLK, bins_total), jnp.float32)
    pad = jnp.zeros((OBLK, bins_total - window), jnp.float32)
    for pb in range(panel_blocks):
        cols = slice(pb * PBLK, (pb + 1) * PBLK)
        seps = [here[:, c : c + 1] - place_ref[c : c + 1, cols] for c in range(3)]
        dist_sq = seps[0] * seps[0] + seps[1] * seps[1] + seps[2] * seps[2]
        parts = [amplitude / jnp.sqrt(dist_sq)] + [amplitude * sep / dist_sq for sep in seps]
        weight = frac_ref[:, cols].astype(jnp.float32)
        low = None
        high = None
        for c in range(4):
            src = src_ref[c, cols, :]
            lo_w = (parts[c] * (1.0 - weight)).astype(jnp.bfloat16)
            hi_w = (parts[c] * weight).astype(jnp.bfloat16)
            lo_p = jnp.dot(lo_w, src, preferred_element_type=jnp.float32)
            hi_p = jnp.dot(hi_w, src, preferred_element_type=jnp.float32)
            low = lo_p if low is None else low + lo_p
            high = hi_p if high is None else high + hi_p
        shift = bins_ref[ob, 0, pb]
        acc = acc + pltpu.roll(jnp.concatenate([low, pad], axis=1), shift, 1)
        acc = acc + pltpu.roll(jnp.concatenate([high, pad], axis=1), shift + 1, 1)
    out_ref[...] = acc.T


def per_device(sources, panel_places, observer_places, fraction, delay_bins, segment_owner):
    local_panels = sources.shape[2]
    window = sources.shape[3]
    bins_total = window + MAXD + 1
    amplitude = 60.0 / math.sqrt(local_panels * lax.axis_size("obs") * lax.axis_size("pan"))
    panel_blocks = local_panels // PBLK
    obs_count = lax.axis_size("obs")
    obs_me = lax.axis_index("obs")
    arrived = [observer_places] + [
        lax.ppermute(observer_places, "obs", [(p, p ^ k) for p in range(obs_count)]) for k in range(1, obs_count)
    ]
    blocks = []
    for q in range(obs_count):
        block = arrived[0]
        for k in range(1, obs_count):
            block = jnp.where((obs_me ^ k) == q, arrived[k], block)
        blocks.append(block)
    every_obs = jnp.concatenate(blocks, axis=1)
    obs_total = every_obs.shape[1]
    obs_blocks = obs_total // OBLK
    kernel = functools.partial(fwh_kernel, amplitude=amplitude, panel_blocks=panel_blocks, window=window, bins_total=bins_total)
    grid_spec = pltpu.PrefetchScalarGridSpec(
        num_scalar_prefetch=1,
        grid=(obs_blocks,),
        in_specs=[
            pl.BlockSpec((3, OBLK), lambda i, b: (0, i)),
            pl.BlockSpec((3, local_panels), lambda i, b: (0, 0)),
            pl.BlockSpec((OBLK, local_panels), lambda i, b: (i, 0)),
            pl.BlockSpec((4, local_panels, window), lambda i, b: (0, 0, 0)),
        ],
        out_specs=pl.BlockSpec((None, bins_total, OBLK), lambda i, b: (i // 2, 0, i % 2)),
    )
    totals = pl.pallas_call(
        kernel,
        grid_spec=grid_spec,
        out_shape=jax.ShapeDtypeStruct((obs_blocks // 2, bins_total, 2 * OBLK), jnp.float32),
    )(delay_bins, every_obs, panel_places[0], fraction[:, 0, :], sources[0])
    halves = totals.reshape((2, 2) + totals.shape[1:])
    me = lax.axis_index("obs")
    for bit, dim in ((0, 1), (1, 0)):
        mine = (me >> bit) & 1
        low = lax.index_in_dim(halves, 0, dim, keepdims=False)
        high = lax.index_in_dim(halves, 1, dim, keepdims=False)
        keep = jnp.where(mine == 1, high, low)
        send = jnp.where(mine == 1, low, high)
        pairs = [(p, p ^ (1 << bit)) for p in range(4)]
        halves = keep + lax.ppermute(send, "obs", pairs)
    reduced = halves
    segment_count = segment_owner.shape[0]
    seg_len = bins_total // segment_count
    arranged = reduced.reshape(segment_count, seg_len, reduced.shape[1])
    inverse = jnp.argsort(segment_owner)
    arranged = arranged[inverse]
    return exchange_sum(arranged)


def exchange_kernel(x_ref, out_ref, slots, send_sem, recv_sem):
    count = x_ref.shape[0]
    me = lax.axis_index("pan")

    def send(d, carry):
        target = lax.rem(me + d, count)
        pltpu.make_async_remote_copy(
            src_ref=x_ref.at[target],
            dst_ref=slots.at[me],
            send_sem=send_sem.at[target],
            recv_sem=recv_sem.at[me],
            device_id={"pan": target},
            device_id_type=pl.DeviceIdType.MESH,
        ).start()
        return carry

    barrier = pltpu.get_barrier_semaphore()

    def knock(d, carry):
        pl.semaphore_signal(barrier, inc=1, device_id={"pan": lax.rem(me + d, count)}, device_id_type=pl.DeviceIdType.MESH)
        return carry

    lax.fori_loop(1, count, knock, 0)
    pl.semaphore_wait(barrier, count - 1)
    lax.fori_loop(1, count, send, 0)
    total = x_ref[me]

    def gather(d, total):
        source = lax.rem(me + count - d, count)
        pltpu.make_async_remote_copy(
            src_ref=x_ref.at[source],
            dst_ref=slots.at[source],
            send_sem=send_sem.at[source],
            recv_sem=recv_sem.at[source],
            device_id={"pan": source},
            device_id_type=pl.DeviceIdType.MESH,
        ).wait_recv()
        return total + slots[source]

    total = lax.fori_loop(1, count, gather, total)

    def drain(d, carry):
        target = lax.rem(me + d, count)
        pltpu.make_async_remote_copy(
            src_ref=x_ref.at[target],
            dst_ref=slots.at[me],
            send_sem=send_sem.at[target],
            recv_sem=recv_sem.at[me],
            device_id={"pan": target},
            device_id_type=pl.DeviceIdType.MESH,
        ).wait_send()
        return carry

    lax.fori_loop(1, count, drain, 0)
    out_ref[...] = total


def exchange_sum(data):
    count = data.shape[0]
    return pl.pallas_call(
        exchange_kernel,
        out_shape=jax.ShapeDtypeStruct(data.shape[1:], data.dtype),
        in_specs=[pl.BlockSpec(memory_space=pltpu.VMEM)],
        out_specs=pl.BlockSpec(memory_space=pltpu.VMEM),
        scratch_shapes=[
            pltpu.VMEM(data.shape, data.dtype),
            pltpu.SemaphoreType.DMA((count,)),
            pltpu.SemaphoreType.DMA((count,)),
        ],
        compiler_params=pltpu.CompilerParams(collective_id=0, has_side_effects=True),
    )(data)


def halving_sum(data, axis, bit_order):
    count = data.shape[0]
    levels = count.bit_length() - 1
    me = lax.axis_index(axis)
    data = data.reshape((2,) * levels + data.shape[1:])
    remaining = list(range(levels - 1, -1, -1))
    for bit in bit_order:
        dim = remaining.index(bit)
        mine = (me >> bit) & 1
        low = lax.index_in_dim(data, 0, dim, keepdims=False)
        high = lax.index_in_dim(data, 1, dim, keepdims=False)
        keep = jnp.where(mine == 1, high, low)
        send = jnp.where(mine == 1, low, high)
        pairs = [(p, p ^ (1 << bit)) for p in range(count)]
        data = keep + lax.ppermute(send, axis, pairs)
        remaining.pop(dim)
    return data


def solution(mesh):
    return jax.shard_map(
        per_device,
        mesh=mesh,
        in_specs=(
            P("pan", None, "obs", None),
            P("pan", None, "obs"),
            P(None, "obs"),
            P(None, "pan", "obs"),
            P(None, "pan", "obs"),
            P(),
        ),
        out_specs=P("pan", "obs"),
        check_vma=False,
    )
```

```python
import functools
import math

import jax
import jax.numpy as jnp
from jax import lax
from jax.experimental import pallas as pl
from jax.experimental.pallas import tpu as pltpu
from jax.sharding import PartitionSpec as P

MAXD = 127
OBLK = 128
PBLK = 128


def fwh_kernel(bins_ref, obs_ref, place_ref, frac_ref, src_ref, out_ref, *, amplitude, panel_blocks, window, bins_total):
    ob = pl.program_id(0)
    here = obs_ref[...].T
    acc = jnp.zeros((OBLK, bins_total), jnp.float32)
    pad = jnp.zeros((OBLK, bins_total - window), jnp.float32)
    for pb in range(panel_blocks):
        cols = slice(pb * PBLK, (pb + 1) * PBLK)
        seps = [here[:, c : c + 1] - place_ref[c : c + 1, cols] for c in range(3)]
        dist_sq = seps[0] * seps[0] + seps[1] * seps[1] + seps[2] * seps[2]
        parts = [amplitude / jnp.sqrt(dist_sq)] + [amplitude * sep / dist_sq for sep in seps]
        weight = frac_ref[:, cols].astype(jnp.float32)
        low = None
        high = None
        for c in range(4):
            src = src_ref[c, cols, :]
            lo_w = (parts[c] * (1.0 - weight)).astype(jnp.bfloat16)
            hi_w = (parts[c] * weight).astype(jnp.bfloat16)
            lo_p = jnp.dot(lo_w, src, preferred_element_type=jnp.float32)
            hi_p = jnp.dot(hi_w, src, preferred_element_type=jnp.float32)
            low = lo_p if low is None else low + lo_p
            high = hi_p if high is None else high + hi_p
        shift = bins_ref[0, pb, ob]
        acc = acc + pltpu.roll(jnp.concatenate([low, pad], axis=1), shift, 1)
        acc = acc + pltpu.roll(jnp.concatenate([high, pad], axis=1), shift + 1, 1)
    out_ref[...] = acc.T


def per_device(sources, panel_places, observer_places, fraction, delay_bins, segment_owner):
    local_panels = sources.shape[2]
    window = sources.shape[3]
    bins_total = window + MAXD + 1
    amplitude = 60.0 / math.sqrt(local_panels * lax.axis_size("obs") * lax.axis_size("pan"))
    panel_blocks = local_panels // PBLK
    obs_count = lax.axis_size("obs")
    obs_me = lax.axis_index("obs")
    arrived = [observer_places] + [
        lax.ppermute(observer_places, "obs", [(p, p ^ k) for p in range(obs_count)]) for k in range(1, obs_count)
    ]
    blocks = []
    for q in range(obs_count):
        block = arrived[0]
        for k in range(1, obs_count):
            block = jnp.where((obs_me ^ k) == q, arrived[k], block)
        blocks.append(block)
    every_obs = jnp.concatenate(blocks, axis=1)
    obs_total = every_obs.shape[1]
    obs_blocks = obs_total // OBLK
    kernel = functools.partial(fwh_kernel, amplitude=amplitude, panel_blocks=panel_blocks, window=window, bins_total=bins_total)
    grid_spec = pltpu.PrefetchScalarGridSpec(
        num_scalar_prefetch=1,
        grid=(obs_blocks,),
        in_specs=[
            pl.BlockSpec((3, OBLK), lambda i, b: (0, i)),
            pl.BlockSpec((3, local_panels), lambda i, b: (0, 0)),
            pl.BlockSpec((OBLK, local_panels), lambda i, b: (i, 0)),
            pl.BlockSpec((4, local_panels, window), lambda i, b: (0, 0, 0)),
        ],
        out_specs=pl.BlockSpec((None, bins_total, OBLK), lambda i, b: (i // 2, 0, i % 2)),
    )
    totals = pl.pallas_call(
        kernel,
        grid_spec=grid_spec,
        out_shape=jax.ShapeDtypeStruct((obs_blocks // 2, bins_total, 2 * OBLK), jnp.float32),
    )(jnp.transpose(delay_bins, (1, 2, 0)), every_obs, panel_places[0], fraction[:, 0, :], sources[0])
    halves = totals.reshape((2, 2) + totals.shape[1:])
    me = lax.axis_index("obs")
    for bit, dim in ((0, 1), (1, 0)):
        mine = (me >> bit) & 1
        low = lax.index_in_dim(halves, 0, dim, keepdims=False)
        high = lax.index_in_dim(halves, 1, dim, keepdims=False)
        keep = jnp.where(mine == 1, high, low)
        send = jnp.where(mine == 1, low, high)
        pairs = [(p, p ^ (1 << bit)) for p in range(4)]
        halves = keep + lax.ppermute(send, "obs", pairs)
    reduced = halves
    segment_count = segment_owner.shape[0]
    seg_len = bins_total // segment_count
    arranged = reduced.reshape(segment_count, seg_len, reduced.shape[1])
    inverse = jnp.argsort(segment_owner)
    arranged = arranged[inverse]
    return exchange_sum(arranged)


def exchange_kernel(x_ref, out_ref, slots, send_sem, recv_sem):
    count = x_ref.shape[0]
    me = lax.axis_index("pan")

    def send(d, carry):
        target = lax.rem(me + d, count)
        pltpu.make_async_remote_copy(
            src_ref=x_ref.at[target],
            dst_ref=slots.at[me],
            send_sem=send_sem.at[target],
            recv_sem=recv_sem.at[me],
            device_id={"pan": target},
            device_id_type=pl.DeviceIdType.MESH,
        ).start()
        return carry

    barrier = pltpu.get_barrier_semaphore()

    def knock(d, carry):
        pl.semaphore_signal(barrier, inc=1, device_id={"pan": lax.rem(me + d, count)}, device_id_type=pl.DeviceIdType.MESH)
        return carry

    lax.fori_loop(1, count, knock, 0)
    pl.semaphore_wait(barrier, count - 1)
    lax.fori_loop(1, count, send, 0)
    total = x_ref[me]

    def gather(d, total):
        source = lax.rem(me + count - d, count)
        pltpu.make_async_remote_copy(
            src_ref=x_ref.at[source],
            dst_ref=slots.at[source],
            send_sem=send_sem.at[source],
            recv_sem=recv_sem.at[source],
            device_id={"pan": source},
            device_id_type=pl.DeviceIdType.MESH,
        ).wait_recv()
        return total + slots[source]

    total = lax.fori_loop(1, count, gather, total)

    def drain(d, carry):
        target = lax.rem(me + d, count)
        pltpu.make_async_remote_copy(
            src_ref=x_ref.at[target],
            dst_ref=slots.at[me],
            send_sem=send_sem.at[target],
            recv_sem=recv_sem.at[me],
            device_id={"pan": target},
            device_id_type=pl.DeviceIdType.MESH,
        ).wait_send()
        return carry

    lax.fori_loop(1, count, drain, 0)
    out_ref[...] = total


def exchange_sum(data):
    count = data.shape[0]
    return pl.pallas_call(
        exchange_kernel,
        out_shape=jax.ShapeDtypeStruct(data.shape[1:], data.dtype),
        in_specs=[pl.BlockSpec(memory_space=pltpu.VMEM)],
        out_specs=pl.BlockSpec(memory_space=pltpu.VMEM),
        scratch_shapes=[
            pltpu.VMEM(data.shape, data.dtype),
            pltpu.SemaphoreType.DMA((count,)),
            pltpu.SemaphoreType.DMA((count,)),
        ],
        compiler_params=pltpu.CompilerParams(collective_id=0, has_side_effects=True),
    )(data)


def halving_sum(data, axis, bit_order):
    count = data.shape[0]
    levels = count.bit_length() - 1
    me = lax.axis_index(axis)
    data = data.reshape((2,) * levels + data.shape[1:])
    remaining = list(range(levels - 1, -1, -1))
    for bit in bit_order:
        dim = remaining.index(bit)
        mine = (me >> bit) & 1
        low = lax.index_in_dim(data, 0, dim, keepdims=False)
        high = lax.index_in_dim(data, 1, dim, keepdims=False)
        keep = jnp.where(mine == 1, high, low)
        send = jnp.where(mine == 1, low, high)
        pairs = [(p, p ^ (1 << bit)) for p in range(count)]
        data = keep + lax.ppermute(send, axis, pairs)
        remaining.pop(dim)
    return data


def solution(mesh):
    return jax.shard_map(
        per_device,
        mesh=mesh,
        in_specs=(
            P("pan", None, "obs", None),
            P("pan", None, "obs"),
            P(None, "obs"),
            P(None, "pan", "obs"),
            P(None, "pan", "obs"),
            P(),
        ),
        out_specs=P("pan", "obs"),
        check_vma=False,
    )
```

```python
import functools
import math

import jax
import jax.numpy as jnp
from jax import lax
from jax.experimental import pallas as pl
from jax.experimental.pallas import tpu as pltpu
from jax.sharding import PartitionSpec as P

MAXD = 127
OBLK = 128
PBLK = 128


def fwh_kernel(bins_ref, obs_ref, place_ref, frac_ref, src_ref, out_ref, *, amplitude, panel_blocks, window, bins_total):
    ob = pl.program_id(0)
    here = obs_ref[...].T
    acc = jnp.zeros((OBLK, bins_total), jnp.float32)
    pad = jnp.zeros((OBLK, bins_total - window), jnp.float32)
    for pb in range(panel_blocks):
        cols = slice(pb * PBLK, (pb + 1) * PBLK)
        seps = [here[:, c : c + 1] - place_ref[c, :, cols] for c in range(3)]
        dist_sq = seps[0] * seps[0] + seps[1] * seps[1] + seps[2] * seps[2]
        parts = [amplitude / jnp.sqrt(dist_sq)] + [amplitude * sep / dist_sq for sep in seps]
        weight = frac_ref[:, cols].astype(jnp.float32)
        low = None
        high = None
        for c in range(4):
            src = src_ref[c, cols, :]
            lo_w = (parts[c] * (1.0 - weight)).astype(jnp.bfloat16)
            hi_w = (parts[c] * weight).astype(jnp.bfloat16)
            lo_p = jnp.dot(lo_w, src, preferred_element_type=jnp.float32)
            hi_p = jnp.dot(hi_w, src, preferred_element_type=jnp.float32)
            low = lo_p if low is None else low + lo_p
            high = hi_p if high is None else high + hi_p
        shift = bins_ref[0, pb, ob]
        acc = acc + pltpu.roll(jnp.concatenate([low, pad], axis=1), shift, 1)
        acc = acc + pltpu.roll(jnp.concatenate([high, pad], axis=1), shift + 1, 1)
    out_ref[...] = acc.T


def per_device(sources, panel_places, observer_places, fraction, delay_bins, segment_owner):
    local_panels = sources.shape[2]
    window = sources.shape[3]
    bins_total = window + MAXD + 1
    amplitude = 60.0 / math.sqrt(local_panels * lax.axis_size("obs") * lax.axis_size("pan"))
    panel_blocks = local_panels // PBLK
    obs_count = lax.axis_size("obs")
    obs_me = lax.axis_index("obs")
    arrived = [observer_places] + [
        lax.ppermute(observer_places, "obs", [(p, p ^ k) for p in range(obs_count)]) for k in range(1, obs_count)
    ]
    blocks = []
    for q in range(obs_count):
        block = arrived[0]
        for k in range(1, obs_count):
            block = jnp.where((obs_me ^ k) == q, arrived[k], block)
        blocks.append(block)
    every_obs = jnp.concatenate(blocks, axis=1)
    obs_total = every_obs.shape[1]
    obs_blocks = obs_total // OBLK
    kernel = functools.partial(fwh_kernel, amplitude=amplitude, panel_blocks=panel_blocks, window=window, bins_total=bins_total)
    grid_spec = pltpu.PrefetchScalarGridSpec(
        num_scalar_prefetch=1,
        grid=(obs_blocks,),
        in_specs=[
            pl.BlockSpec((3, OBLK), lambda i, b: (0, i)),
            pl.BlockSpec((3, 1, local_panels), lambda i, b: (0, 0, 0)),
            pl.BlockSpec((OBLK, local_panels), lambda i, b: (i, 0)),
            pl.BlockSpec((4, local_panels, window), lambda i, b: (0, 0, 0)),
        ],
        out_specs=pl.BlockSpec((None, bins_total, OBLK), lambda i, b: (i // 2, 0, i % 2)),
    )
    totals = pl.pallas_call(
        kernel,
        grid_spec=grid_spec,
        out_shape=jax.ShapeDtypeStruct((obs_blocks // 2, bins_total, 2 * OBLK), jnp.float32),
    )(jnp.transpose(delay_bins, (1, 2, 0)), every_obs, jnp.transpose(panel_places, (1, 0, 2)), fraction[:, 0, :], sources[0])
    halves = totals.reshape((2, 2) + totals.shape[1:])
    me = lax.axis_index("obs")
    for bit, dim in ((0, 1), (1, 0)):
        mine = (me >> bit) & 1
        low = lax.index_in_dim(halves, 0, dim, keepdims=False)
        high = lax.index_in_dim(halves, 1, dim, keepdims=False)
        keep = jnp.where(mine == 1, high, low)
        send = jnp.where(mine == 1, low, high)
        pairs = [(p, p ^ (1 << bit)) for p in range(4)]
        halves = keep + lax.ppermute(send, "obs", pairs)
    reduced = halves
    segment_count = segment_owner.shape[0]
    seg_len = bins_total // segment_count
    arranged = reduced.reshape(segment_count, seg_len, reduced.shape[1])
    inverse = jnp.argsort(segment_owner)
    arranged = arranged[inverse]
    return exchange_sum(arranged)


def exchange_kernel(x_ref, out_ref, slots, send_sem, recv_sem):
    count = x_ref.shape[0]
    me = lax.axis_index("pan")

    def send(d, carry):
        target = lax.rem(me + d, count)
        pltpu.make_async_remote_copy(
            src_ref=x_ref.at[target],
            dst_ref=slots.at[me],
            send_sem=send_sem.at[target],
            recv_sem=recv_sem.at[me],
            device_id={"pan": target},
            device_id_type=pl.DeviceIdType.MESH,
        ).start()
        return carry

    barrier = pltpu.get_barrier_semaphore()

    def knock(d, carry):
        pl.semaphore_signal(barrier, inc=1, device_id={"pan": lax.rem(me + d, count)}, device_id_type=pl.DeviceIdType.MESH)
        return carry

    lax.fori_loop(1, count, knock, 0)
    pl.semaphore_wait(barrier, count - 1)
    lax.fori_loop(1, count, send, 0)
    total = x_ref[me]

    def gather(d, total):
        source = lax.rem(me + count - d, count)
        pltpu.make_async_remote_copy(
            src_ref=x_ref.at[source],
            dst_ref=slots.at[source],
            send_sem=send_sem.at[source],
            recv_sem=recv_sem.at[source],
            device_id={"pan": source},
            device_id_type=pl.DeviceIdType.MESH,
        ).wait_recv()
        return total + slots[source]

    total = lax.fori_loop(1, count, gather, total)

    def drain(d, carry):
        target = lax.rem(me + d, count)
        pltpu.make_async_remote_copy(
            src_ref=x_ref.at[target],
            dst_ref=slots.at[me],
            send_sem=send_sem.at[target],
            recv_sem=recv_sem.at[me],
            device_id={"pan": target},
            device_id_type=pl.DeviceIdType.MESH,
        ).wait_send()
        return carry

    lax.fori_loop(1, count, drain, 0)
    out_ref[...] = total


def exchange_sum(data):
    count = data.shape[0]
    return pl.pallas_call(
        exchange_kernel,
        out_shape=jax.ShapeDtypeStruct(data.shape[1:], data.dtype),
        in_specs=[pl.BlockSpec(memory_space=pltpu.VMEM)],
        out_specs=pl.BlockSpec(memory_space=pltpu.VMEM),
        scratch_shapes=[
            pltpu.VMEM(data.shape, data.dtype),
            pltpu.SemaphoreType.DMA((count,)),
            pltpu.SemaphoreType.DMA((count,)),
        ],
        compiler_params=pltpu.CompilerParams(collective_id=0, has_side_effects=True),
    )(data)


def halving_sum(data, axis, bit_order):
    count = data.shape[0]
    levels = count.bit_length() - 1
    me = lax.axis_index(axis)
    data = data.reshape((2,) * levels + data.shape[1:])
    remaining = list(range(levels - 1, -1, -1))
    for bit in bit_order:
        dim = remaining.index(bit)
        mine = (me >> bit) & 1
        low = lax.index_in_dim(data, 0, dim, keepdims=False)
        high = lax.index_in_dim(data, 1, dim, keepdims=False)
        keep = jnp.where(mine == 1, high, low)
        send = jnp.where(mine == 1, low, high)
        pairs = [(p, p ^ (1 << bit)) for p in range(count)]
        data = keep + lax.ppermute(send, axis, pairs)
        remaining.pop(dim)
    return data


def solution(mesh):
    return jax.shard_map(
        per_device,
        mesh=mesh,
        in_specs=(
            P("pan", None, "obs", None),
            P("pan", None, "obs"),
            P(None, "obs"),
            P(None, "pan", "obs"),
            P(None, "pan", "obs"),
            P(),
        ),
        out_specs=P("pan", "obs"),
        check_vma=False,
    )
```

```python
import functools
import math

import jax
import jax.numpy as jnp
from jax import lax
from jax.experimental import pallas as pl
from jax.experimental.pallas import tpu as pltpu
from jax.sharding import PartitionSpec as P

MAXD = 127
OBLK = 128
PBLK = 128


def fwh_kernel(bins_ref, obs_ref, place_ref, frac_ref, src_ref, out_ref, *, amplitude, panel_blocks, window, bins_total):
    ob = pl.program_id(0)
    here = obs_ref[...].T
    acc = jnp.zeros((OBLK, bins_total), jnp.float32)
    pad = jnp.zeros((OBLK, bins_total - window), jnp.float32)
    for pb in range(panel_blocks):
        cols = slice(pb * PBLK, (pb + 1) * PBLK)
        seps = [here[:, c : c + 1] - place_ref[c : c + 1, cols] for c in range(3)]
        dist_sq = seps[0] * seps[0] + seps[1] * seps[1] + seps[2] * seps[2]
        inverse = 1.0 / dist_sq
        parts = [amplitude / jnp.sqrt(dist_sq)] + [(amplitude * sep) * inverse for sep in seps]
        weight = frac_ref[:, cols].astype(jnp.float32)
        rest = 1.0 - weight
        lo_w = jnp.concatenate([(part * rest).astype(jnp.bfloat16) for part in parts], axis=1)
        hi_w = jnp.concatenate([(part * weight).astype(jnp.bfloat16) for part in parts], axis=1)
        src = src_ref[:, cols, :].reshape(4 * PBLK, src_ref.shape[2])
        low = jnp.dot(lo_w, src, preferred_element_type=jnp.float32)
        high = jnp.dot(hi_w, src, preferred_element_type=jnp.float32)
        shift = bins_ref[0, pb, ob]
        acc = acc + pltpu.roll(jnp.concatenate([low, pad], axis=1), shift, 1)
        acc = acc + pltpu.roll(jnp.concatenate([high, pad], axis=1), shift + 1, 1)
    out_ref[...] = acc.T


def per_device(sources, panel_places, observer_places, fraction, delay_bins, segment_owner):
    local_panels = sources.shape[2]
    window = sources.shape[3]
    bins_total = window + MAXD + 1
    amplitude = 60.0 / math.sqrt(local_panels * lax.axis_size("obs") * lax.axis_size("pan"))
    panel_blocks = local_panels // PBLK
    obs_count = lax.axis_size("obs")
    obs_me = lax.axis_index("obs")
    arrived = [observer_places] + [
        lax.ppermute(observer_places, "obs", [(p, p ^ k) for p in range(obs_count)]) for k in range(1, obs_count)
    ]
    blocks = []
    for q in range(obs_count):
        block = arrived[0]
        for k in range(1, obs_count):
            block = jnp.where((obs_me ^ k) == q, arrived[k], block)
        blocks.append(block)
    every_obs = jnp.concatenate(blocks, axis=1)
    obs_total = every_obs.shape[1]
    obs_blocks = obs_total // OBLK
    kernel = functools.partial(fwh_kernel, amplitude=amplitude, panel_blocks=panel_blocks, window=window, bins_total=bins_total)
    grid_spec = pltpu.PrefetchScalarGridSpec(
        num_scalar_prefetch=1,
        grid=(obs_blocks,),
        in_specs=[
            pl.BlockSpec((3, OBLK), lambda i, b: (0, i)),
            pl.BlockSpec((3, local_panels), lambda i, b: (0, 0)),
            pl.BlockSpec((OBLK, local_panels), lambda i, b: (i, 0)),
            pl.BlockSpec((4, local_panels, window), lambda i, b: (0, 0, 0)),
        ],
        out_specs=pl.BlockSpec((None, bins_total, OBLK), lambda i, b: (i // 2, 0, i % 2)),
    )
    totals = pl.pallas_call(
        kernel,
        grid_spec=grid_spec,
        out_shape=jax.ShapeDtypeStruct((obs_blocks // 2, bins_total, 2 * OBLK), jnp.float32),
    )(jnp.transpose(delay_bins, (1, 2, 0)), every_obs, panel_places[0], fraction[:, 0, :], sources[0])
    halves = totals.reshape((2, 2) + totals.shape[1:])
    me = lax.axis_index("obs")
    for bit, dim in ((0, 1), (1, 0)):
        mine = (me >> bit) & 1
        low = lax.index_in_dim(halves, 0, dim, keepdims=False)
        high = lax.index_in_dim(halves, 1, dim, keepdims=False)
        keep = jnp.where(mine == 1, high, low)
        send = jnp.where(mine == 1, low, high)
        pairs = [(p, p ^ (1 << bit)) for p in range(4)]
        halves = keep + lax.ppermute(send, "obs", pairs)
    reduced = halves
    segment_count = segment_owner.shape[0]
    seg_len = bins_total // segment_count
    arranged = reduced.reshape(segment_count, seg_len, reduced.shape[1])
    inverse = jnp.argsort(segment_owner)
    arranged = arranged[inverse]
    return exchange_sum(arranged)


def exchange_kernel(x_ref, out_ref, slots, send_sem, recv_sem):
    count = x_ref.shape[0]
    me = lax.axis_index("pan")

    def send(d, carry):
        target = lax.rem(me + d, count)
        pltpu.make_async_remote_copy(
            src_ref=x_ref.at[target],
            dst_ref=slots.at[me],
            send_sem=send_sem.at[target],
            recv_sem=recv_sem.at[me],
            device_id={"pan": target},
            device_id_type=pl.DeviceIdType.MESH,
        ).start()
        return carry

    barrier = pltpu.get_barrier_semaphore()

    def knock(d, carry):
        pl.semaphore_signal(barrier, inc=1, device_id={"pan": lax.rem(me + d, count)}, device_id_type=pl.DeviceIdType.MESH)
        return carry

    lax.fori_loop(1, count, knock, 0)
    pl.semaphore_wait(barrier, count - 1)
    lax.fori_loop(1, count, send, 0)
    total = x_ref[me]

    def gather(d, total):
        source = lax.rem(me + count - d, count)
        pltpu.make_async_remote_copy(
            src_ref=x_ref.at[source],
            dst_ref=slots.at[source],
            send_sem=send_sem.at[source],
            recv_sem=recv_sem.at[source],
            device_id={"pan": source},
            device_id_type=pl.DeviceIdType.MESH,
        ).wait_recv()
        return total + slots[source]

    total = lax.fori_loop(1, count, gather, total)

    def drain(d, carry):
        target = lax.rem(me + d, count)
        pltpu.make_async_remote_copy(
            src_ref=x_ref.at[target],
            dst_ref=slots.at[me],
            send_sem=send_sem.at[target],
            recv_sem=recv_sem.at[me],
            device_id={"pan": target},
            device_id_type=pl.DeviceIdType.MESH,
        ).wait_send()
        return carry

    lax.fori_loop(1, count, drain, 0)
    out_ref[...] = total


def exchange_sum(data):
    count = data.shape[0]
    return pl.pallas_call(
        exchange_kernel,
        out_shape=jax.ShapeDtypeStruct(data.shape[1:], data.dtype),
        in_specs=[pl.BlockSpec(memory_space=pltpu.VMEM)],
        out_specs=pl.BlockSpec(memory_space=pltpu.VMEM),
        scratch_shapes=[
            pltpu.VMEM(data.shape, data.dtype),
            pltpu.SemaphoreType.DMA((count,)),
            pltpu.SemaphoreType.DMA((count,)),
        ],
        compiler_params=pltpu.CompilerParams(collective_id=0, has_side_effects=True),
    )(data)


def halving_sum(data, axis, bit_order):
    count = data.shape[0]
    levels = count.bit_length() - 1
    me = lax.axis_index(axis)
    data = data.reshape((2,) * levels + data.shape[1:])
    remaining = list(range(levels - 1, -1, -1))
    for bit in bit_order:
        dim = remaining.index(bit)
        mine = (me >> bit) & 1
        low = lax.index_in_dim(data, 0, dim, keepdims=False)
        high = lax.index_in_dim(data, 1, dim, keepdims=False)
        keep = jnp.where(mine == 1, high, low)
        send = jnp.where(mine == 1, low, high)
        pairs = [(p, p ^ (1 << bit)) for p in range(count)]
        data = keep + lax.ppermute(send, axis, pairs)
        remaining.pop(dim)
    return data


def solution(mesh):
    return jax.shard_map(
        per_device,
        mesh=mesh,
        in_specs=(
            P("pan", None, "obs", None),
            P("pan", None, "obs"),
            P(None, "obs"),
            P(None, "pan", "obs"),
            P(None, "pan", "obs"),
            P(),
        ),
        out_specs=P("pan", "obs"),
        check_vma=False,
    )
```

```python
import functools
import math

import jax
import jax.numpy as jnp
from jax import lax
from jax.experimental import pallas as pl
from jax.experimental.pallas import tpu as pltpu
from jax.sharding import PartitionSpec as P

MAXD = 127
OBLK = 128
PBLK = 128


def fwh_kernel(bins_ref, obs_ref, place_ref, frac_ref, src_ref, out_ref, *, amplitude, panel_blocks, window, bins_total):
    ob = pl.program_id(0)
    here = obs_ref[...].T
    acc = jnp.zeros((OBLK, bins_total), jnp.float32)
    pad = jnp.zeros((OBLK, bins_total - window), jnp.float32)
    for pb in range(panel_blocks):
        cols = slice(pb * PBLK, (pb + 1) * PBLK)
        seps = [here[:, c : c + 1] - place_ref[c : c + 1, cols] for c in range(3)]
        dist_sq = seps[0] * seps[0] + seps[1] * seps[1] + seps[2] * seps[2]
        inverse = 1.0 / dist_sq
        parts = [amplitude / jnp.sqrt(dist_sq)] + [(amplitude * sep) * inverse for sep in seps]
        weight = frac_ref[:, cols].astype(jnp.float32)
        rest = 1.0 - weight
        lo_w = jnp.concatenate([(part * rest).astype(jnp.bfloat16) for part in parts], axis=1)
        hi_w = jnp.concatenate([(part * weight).astype(jnp.bfloat16) for part in parts], axis=1)
        src = src_ref[:, cols, :].reshape(4 * PBLK, src_ref.shape[2])
        low = jnp.dot(lo_w, src, preferred_element_type=jnp.float32)
        high = jnp.dot(hi_w, src, preferred_element_type=jnp.float32)
        shift = bins_ref[0, pb, ob]
        acc = acc + pltpu.roll(jnp.concatenate([low, pad], axis=1), shift, 1)
        acc = acc + pltpu.roll(jnp.concatenate([high, pad], axis=1), shift + 1, 1)
    out_ref[...] = acc.T


def per_device(sources, panel_places, observer_places, fraction, delay_bins, segment_owner):
    local_panels = sources.shape[2]
    window = sources.shape[3]
    bins_total = window + MAXD + 1
    amplitude = 60.0 / math.sqrt(local_panels * lax.axis_size("obs") * lax.axis_size("pan"))
    panel_blocks = local_panels // PBLK
    obs_count = lax.axis_size("obs")
    obs_me = lax.axis_index("obs")
    arrived = [observer_places] + [
        lax.ppermute(observer_places, "obs", [(p, p ^ k) for p in range(obs_count)]) for k in range(1, obs_count)
    ]
    blocks = []
    for q in range(obs_count):
        block = arrived[0]
        for k in range(1, obs_count):
            block = jnp.where((obs_me ^ k) == q, arrived[k], block)
        blocks.append(block)
    every_obs = jnp.concatenate(blocks, axis=1)
    obs_total = every_obs.shape[1]
    obs_blocks = obs_total // OBLK
    kernel = functools.partial(fwh_kernel, amplitude=amplitude, panel_blocks=panel_blocks, window=window, bins_total=bins_total)
    grid_spec = pltpu.PrefetchScalarGridSpec(
        num_scalar_prefetch=1,
        grid=(obs_blocks,),
        in_specs=[
            pl.BlockSpec((3, OBLK), lambda i, b: (0, i)),
            pl.BlockSpec((3, local_panels), lambda i, b: (0, 0)),
            pl.BlockSpec((OBLK, local_panels), lambda i, b: (i, 0)),
            pl.BlockSpec((4, local_panels, window), lambda i, b: (0, 0, 0)),
        ],
        out_specs=pl.BlockSpec((None, bins_total, OBLK), lambda i, b: (i // 2, 0, i % 2)),
    )
    totals = pl.pallas_call(
        kernel,
        grid_spec=grid_spec,
        out_shape=jax.ShapeDtypeStruct((obs_blocks // 2, bins_total, 2 * OBLK), jnp.float32),
    )(jnp.transpose(delay_bins, (1, 2, 0)), every_obs, panel_places[0], fraction[:, 0, :], sources[0])
    halves = totals.reshape((2, 2) + totals.shape[1:])
    me = lax.axis_index("obs")
    mine = me & 1
    low = halves[:, 0]
    high = halves[:, 1]
    keep = jnp.where(mine == 1, high, low)
    send = jnp.where(mine == 1, low, high)
    halves = keep + lax.ppermute(send, "obs", [(p, p ^ 1) for p in range(4)])
    segment_count = segment_owner.shape[0]
    seg_len = bins_total // segment_count
    arranged = halves.reshape(2, segment_count, seg_len, halves.shape[2])
    inverse = jnp.argsort(segment_owner)
    arranged = jnp.swapaxes(arranged[:, inverse], 0, 1)
    summed = exchange_sum(arranged)
    upper = (me >> 1) & 1
    keep = jnp.where(upper == 1, summed[1], summed[0])
    send = jnp.where(upper == 1, summed[0], summed[1])
    return keep + lax.ppermute(send, "obs", [(p, p ^ 2) for p in range(4)])


def exchange_kernel(x_ref, out_ref, slots, send_sem, recv_sem):
    count = x_ref.shape[0]
    me = lax.axis_index("pan")

    def send(d, carry):
        target = lax.rem(me + d, count)
        pltpu.make_async_remote_copy(
            src_ref=x_ref.at[target],
            dst_ref=slots.at[me],
            send_sem=send_sem.at[target],
            recv_sem=recv_sem.at[me],
            device_id={"pan": target},
            device_id_type=pl.DeviceIdType.MESH,
        ).start()
        return carry

    barrier = pltpu.get_barrier_semaphore()

    def knock(d, carry):
        pl.semaphore_signal(barrier, inc=1, device_id={"pan": lax.rem(me + d, count)}, device_id_type=pl.DeviceIdType.MESH)
        return carry

    lax.fori_loop(1, count, knock, 0)
    pl.semaphore_wait(barrier, count - 1)
    lax.fori_loop(1, count, send, 0)
    total = x_ref[me]

    def gather(d, total):
        source = lax.rem(me + count - d, count)
        pltpu.make_async_remote_copy(
            src_ref=x_ref.at[source],
            dst_ref=slots.at[source],
            send_sem=send_sem.at[source],
            recv_sem=recv_sem.at[source],
            device_id={"pan": source},
            device_id_type=pl.DeviceIdType.MESH,
        ).wait_recv()
        return total + slots[source]

    total = lax.fori_loop(1, count, gather, total)

    def drain(d, carry):
        target = lax.rem(me + d, count)
        pltpu.make_async_remote_copy(
            src_ref=x_ref.at[target],
            dst_ref=slots.at[me],
            send_sem=send_sem.at[target],
            recv_sem=recv_sem.at[me],
            device_id={"pan": target},
            device_id_type=pl.DeviceIdType.MESH,
        ).wait_send()
        return carry

    lax.fori_loop(1, count, drain, 0)
    out_ref[...] = total


def exchange_sum(data):
    count = data.shape[0]
    return pl.pallas_call(
        exchange_kernel,
        out_shape=jax.ShapeDtypeStruct(data.shape[1:], data.dtype),
        in_specs=[pl.BlockSpec(memory_space=pltpu.VMEM)],
        out_specs=pl.BlockSpec(memory_space=pltpu.VMEM),
        scratch_shapes=[
            pltpu.VMEM(data.shape, data.dtype),
            pltpu.SemaphoreType.DMA((count,)),
            pltpu.SemaphoreType.DMA((count,)),
        ],
        compiler_params=pltpu.CompilerParams(collective_id=0, has_side_effects=True),
    )(data)


def halving_sum(data, axis, bit_order):
    count = data.shape[0]
    levels = count.bit_length() - 1
    me = lax.axis_index(axis)
    data = data.reshape((2,) * levels + data.shape[1:])
    remaining = list(range(levels - 1, -1, -1))
    for bit in bit_order:
        dim = remaining.index(bit)
        mine = (me >> bit) & 1
        low = lax.index_in_dim(data, 0, dim, keepdims=False)
        high = lax.index_in_dim(data, 1, dim, keepdims=False)
        keep = jnp.where(mine == 1, high, low)
        send = jnp.where(mine == 1, low, high)
        pairs = [(p, p ^ (1 << bit)) for p in range(count)]
        data = keep + lax.ppermute(send, axis, pairs)
        remaining.pop(dim)
    return data


def solution(mesh):
    return jax.shard_map(
        per_device,
        mesh=mesh,
        in_specs=(
            P("pan", None, "obs", None),
            P("pan", None, "obs"),
            P(None, "obs"),
            P(None, "pan", "obs"),
            P(None, "pan", "obs"),
            P(),
        ),
        out_specs=P("pan", "obs"),
        check_vma=False,
    )
```

```python
import functools
import math

import jax
import jax.numpy as jnp
from jax import lax
from jax.experimental import pallas as pl
from jax.experimental.pallas import tpu as pltpu
from jax.sharding import PartitionSpec as P

MAXD = 127
OBLK = 128
PBLK = 128


def fwh_kernel(bins_ref, obs_ref, place_ref, frac_ref, src_ref, out_ref, *, amplitude, panel_blocks, window, bins_total):
    ob = pl.program_id(0)
    here = obs_ref[...].T
    acc = jnp.zeros((OBLK, bins_total), jnp.float32)
    pad = jnp.zeros((OBLK, bins_total - window), jnp.float32)
    for pb in range(panel_blocks):
        cols = slice(pb * PBLK, (pb + 1) * PBLK)
        seps = [here[:, c : c + 1] - place_ref[c : c + 1, cols] for c in range(3)]
        dist_sq = seps[0] * seps[0] + seps[1] * seps[1] + seps[2] * seps[2]
        inverse = 1.0 / dist_sq
        parts = [amplitude / jnp.sqrt(dist_sq)] + [(amplitude * sep) * inverse for sep in seps]
        weight = frac_ref[:, cols].astype(jnp.float32)
        rest = 1.0 - weight
        lo_w = jnp.concatenate([(part * rest).astype(jnp.bfloat16) for part in parts], axis=1)
        hi_w = jnp.concatenate([(part * weight).astype(jnp.bfloat16) for part in parts], axis=1)
        src = src_ref[:, cols, :].reshape(4 * PBLK, src_ref.shape[2])
        low = jnp.dot(lo_w, src, preferred_element_type=jnp.float32)
        high = jnp.dot(hi_w, src, preferred_element_type=jnp.float32)
        shift = bins_ref[0, pb, ob]
        acc = acc + pltpu.roll(jnp.concatenate([low, pad], axis=1), shift, 1)
        acc = acc + pltpu.roll(jnp.concatenate([high, pad], axis=1), shift + 1, 1)
    out_ref[...] = acc.T


def per_device(sources, panel_places, observer_places, fraction, delay_bins, segment_owner):
    local_panels = sources.shape[2]
    window = sources.shape[3]
    bins_total = window + MAXD + 1
    amplitude = 60.0 / math.sqrt(local_panels * lax.axis_size("obs") * lax.axis_size("pan"))
    panel_blocks = local_panels // PBLK
    obs_count = lax.axis_size("obs")
    obs_me = lax.axis_index("obs")
    arrived = [observer_places] + [
        lax.ppermute(observer_places, "obs", [(p, p ^ k) for p in range(obs_count)]) for k in range(1, obs_count)
    ]
    blocks = []
    for q in range(obs_count):
        block = arrived[0]
        for k in range(1, obs_count):
            block = jnp.where((obs_me ^ k) == q, arrived[k], block)
        blocks.append(block)
    every_obs = jnp.concatenate(blocks, axis=1)
    obs_total = every_obs.shape[1]
    obs_blocks = obs_total // OBLK
    kernel = functools.partial(fwh_kernel, amplitude=amplitude, panel_blocks=panel_blocks, window=window, bins_total=bins_total)
    grid_spec = pltpu.PrefetchScalarGridSpec(
        num_scalar_prefetch=1,
        grid=(obs_blocks,),
        in_specs=[
            pl.BlockSpec((3, OBLK), lambda i, b: (0, i)),
            pl.BlockSpec((3, local_panels), lambda i, b: (0, 0)),
            pl.BlockSpec((OBLK, local_panels), lambda i, b: (i, 0)),
            pl.BlockSpec((4, local_panels, window), lambda i, b: (0, 0, 0)),
        ],
        out_specs=pl.BlockSpec((None, bins_total, OBLK), lambda i, b: (i // 2, 0, i % 2)),
    )
    totals = pl.pallas_call(
        kernel,
        grid_spec=grid_spec,
        out_shape=jax.ShapeDtypeStruct((obs_blocks // 2, bins_total, 2 * OBLK), jnp.float32),
    )(jnp.transpose(delay_bins, (1, 2, 0)), every_obs, panel_places[0], fraction[:, 0, :], sources[0])
    halves = totals.reshape((2, 2) + totals.shape[1:])
    me = lax.axis_index("obs")
    for bit, dim in ((0, 1), (1, 0)):
        mine = (me >> bit) & 1
        low = lax.index_in_dim(halves, 0, dim, keepdims=False)
        high = lax.index_in_dim(halves, 1, dim, keepdims=False)
        keep = jnp.where(mine == 1, high, low)
        send = jnp.where(mine == 1, low, high)
        pairs = [(p, p ^ (1 << bit)) for p in range(4)]
        halves = keep + lax.ppermute(send, "obs", pairs)
    reduced = halves
    segment_count = segment_owner.shape[0]
    seg_len = bins_total // segment_count
    arranged = reduced.reshape(segment_count, seg_len, reduced.shape[1])
    inverse = jnp.argsort(segment_owner)
    arranged = arranged[inverse]
    flat = arranged.reshape(segment_count, 1, seg_len * arranged.shape[2])
    return exchange_sum(flat).reshape(seg_len, arranged.shape[2])


def exchange_kernel(x_ref, out_ref, slots, send_sem, recv_sem):
    count = x_ref.shape[0]
    me = lax.axis_index("pan")

    def send(d, carry):
        target = lax.rem(me + d, count)
        pltpu.make_async_remote_copy(
            src_ref=x_ref.at[target],
            dst_ref=slots.at[me],
            send_sem=send_sem.at[target],
            recv_sem=recv_sem.at[me],
            device_id={"pan": target},
            device_id_type=pl.DeviceIdType.MESH,
        ).start()
        return carry

    barrier = pltpu.get_barrier_semaphore()

    def knock(d, carry):
        pl.semaphore_signal(barrier, inc=1, device_id={"pan": lax.rem(me + d, count)}, device_id_type=pl.DeviceIdType.MESH)
        return carry

    lax.fori_loop(1, count, knock, 0)
    pl.semaphore_wait(barrier, count - 1)
    lax.fori_loop(1, count, send, 0)
    total = x_ref[me]

    def gather(d, total):
        source = lax.rem(me + count - d, count)
        pltpu.make_async_remote_copy(
            src_ref=x_ref.at[source],
            dst_ref=slots.at[source],
            send_sem=send_sem.at[source],
            recv_sem=recv_sem.at[source],
            device_id={"pan": source},
            device_id_type=pl.DeviceIdType.MESH,
        ).wait_recv()
        return total + slots[source]

    total = lax.fori_loop(1, count, gather, total)

    def drain(d, carry):
        target = lax.rem(me + d, count)
        pltpu.make_async_remote_copy(
            src_ref=x_ref.at[target],
            dst_ref=slots.at[me],
            send_sem=send_sem.at[target],
            recv_sem=recv_sem.at[me],
            device_id={"pan": target},
            device_id_type=pl.DeviceIdType.MESH,
        ).wait_send()
        return carry

    lax.fori_loop(1, count, drain, 0)
    out_ref[...] = total


def exchange_sum(data):
    count = data.shape[0]
    return pl.pallas_call(
        exchange_kernel,
        out_shape=jax.ShapeDtypeStruct(data.shape[1:], data.dtype),
        in_specs=[pl.BlockSpec(memory_space=pltpu.VMEM)],
        out_specs=pl.BlockSpec(memory_space=pltpu.VMEM),
        scratch_shapes=[
            pltpu.VMEM(data.shape, data.dtype),
            pltpu.SemaphoreType.DMA((count,)),
            pltpu.SemaphoreType.DMA((count,)),
        ],
        compiler_params=pltpu.CompilerParams(collective_id=0, has_side_effects=True),
    )(data)


def halving_sum(data, axis, bit_order):
    count = data.shape[0]
    levels = count.bit_length() - 1
    me = lax.axis_index(axis)
    data = data.reshape((2,) * levels + data.shape[1:])
    remaining = list(range(levels - 1, -1, -1))
    for bit in bit_order:
        dim = remaining.index(bit)
        mine = (me >> bit) & 1
        low = lax.index_in_dim(data, 0, dim, keepdims=False)
        high = lax.index_in_dim(data, 1, dim, keepdims=False)
        keep = jnp.where(mine == 1, high, low)
        send = jnp.where(mine == 1, low, high)
        pairs = [(p, p ^ (1 << bit)) for p in range(count)]
        data = keep + lax.ppermute(send, axis, pairs)
        remaining.pop(dim)
    return data


def solution(mesh):
    return jax.shard_map(
        per_device,
        mesh=mesh,
        in_specs=(
            P("pan", None, "obs", None),
            P("pan", None, "obs"),
            P(None, "obs"),
            P(None, "pan", "obs"),
            P(None, "pan", "obs"),
            P(),
        ),
        out_specs=P("pan", "obs"),
        check_vma=False,
    )
```

```python
import functools
import math

import jax
import jax.numpy as jnp
from jax import lax
from jax.experimental import pallas as pl
from jax.experimental.pallas import tpu as pltpu
from jax.sharding import PartitionSpec as P

MAXD = 127
OBLK = 128
PBLK = 128


def fwh_kernel(bins_ref, me_ref, obs_ref, place_ref, frac_ref, src_ref, out_ref, *, amplitude, panel_blocks, window, bins_total):
    ob = pl.program_id(0)
    here = obs_ref[...].T
    acc = jnp.zeros((OBLK, bins_total), jnp.float32)
    pad = jnp.zeros((OBLK, bins_total - window), jnp.float32)
    for pb in range(panel_blocks):
        cols = slice(pb * PBLK, (pb + 1) * PBLK)
        seps = [here[:, c : c + 1] - place_ref[c : c + 1, cols] for c in range(3)]
        dist_sq = seps[0] * seps[0] + seps[1] * seps[1] + seps[2] * seps[2]
        inverse = 1.0 / dist_sq
        parts = [amplitude / jnp.sqrt(dist_sq)] + [(amplitude * sep) * inverse for sep in seps]
        weight = frac_ref[:, cols].astype(jnp.float32)
        rest = 1.0 - weight
        lo_w = jnp.concatenate([(part * rest).astype(jnp.bfloat16) for part in parts], axis=1)
        hi_w = jnp.concatenate([(part * weight).astype(jnp.bfloat16) for part in parts], axis=1)
        src = src_ref[:, cols, :].reshape(4 * PBLK, src_ref.shape[2])
        low = jnp.dot(lo_w, src, preferred_element_type=jnp.float32)
        high = jnp.dot(hi_w, src, preferred_element_type=jnp.float32)
        shift = bins_ref[0, pb, ob]
        acc = acc + pltpu.roll(jnp.concatenate([low, pad], axis=1), shift, 1)
        acc = acc + pltpu.roll(jnp.concatenate([high, pad], axis=1), shift + 1, 1)
    out_ref[...] = acc.T


def per_device(sources, panel_places, observer_places, fraction, delay_bins, segment_owner):
    local_panels = sources.shape[2]
    window = sources.shape[3]
    bins_total = window + MAXD + 1
    amplitude = 60.0 / math.sqrt(local_panels * lax.axis_size("obs") * lax.axis_size("pan"))
    panel_blocks = local_panels // PBLK
    obs_count = lax.axis_size("obs")
    obs_me = lax.axis_index("obs")
    arrived = [observer_places] + [
        lax.ppermute(observer_places, "obs", [(p, p ^ k) for p in range(obs_count)]) for k in range(1, obs_count)
    ]
    blocks = []
    for q in range(obs_count):
        block = arrived[0]
        for k in range(1, obs_count):
            block = jnp.where((obs_me ^ k) == q, arrived[k], block)
        blocks.append(block)
    every_obs = jnp.concatenate(blocks, axis=1)
    obs_total = every_obs.shape[1]
    obs_blocks = obs_total // OBLK
    kernel = functools.partial(fwh_kernel, amplitude=amplitude, panel_blocks=panel_blocks, window=window, bins_total=bins_total)
    grid_spec = pltpu.PrefetchScalarGridSpec(
        num_scalar_prefetch=2,
        grid=(obs_blocks,),
        in_specs=[
            pl.BlockSpec((3, OBLK), lambda i, b, m: (0, i)),
            pl.BlockSpec((3, local_panels), lambda i, b, m: (0, 0)),
            pl.BlockSpec((OBLK, local_panels), lambda i, b, m: (i, 0)),
            pl.BlockSpec((4, local_panels, window), lambda i, b, m: (0, 0, 0)),
        ],
        out_specs=pl.BlockSpec((None, bins_total, OBLK), lambda i, b, m: (((i // 2) % 2 + m[0]) % 2 * 2 + ((i // 4) + m[0] // 2) % 2, 0, i % 2)),
    )
    totals = pl.pallas_call(
        kernel,
        grid_spec=grid_spec,
        out_shape=jax.ShapeDtypeStruct((obs_blocks // 2, bins_total, 2 * OBLK), jnp.float32),
    )(jnp.transpose(delay_bins, (1, 2, 0)), jnp.reshape(obs_me, (1,)).astype(jnp.int32), every_obs, panel_places[0], fraction[:, 0, :], sources[0])
    halves = totals.reshape((2, 2) + totals.shape[1:])
    for bit in (0, 1):
        pairs = [(p, p ^ (1 << bit)) for p in range(4)]
        halves = halves[0] + lax.ppermute(halves[1], "obs", pairs)
    reduced = halves
    segment_count = segment_owner.shape[0]
    seg_len = bins_total // segment_count
    arranged = reduced.reshape(segment_count, seg_len, reduced.shape[1])
    inverse = jnp.argsort(segment_owner)
    arranged = arranged[inverse]
    flat = arranged.reshape(segment_count, 1, seg_len * arranged.shape[2])
    return exchange_sum(flat).reshape(seg_len, arranged.shape[2])


def exchange_kernel(x_ref, out_ref, slots, send_sem, recv_sem):
    count = x_ref.shape[0]
    me = lax.axis_index("pan")

    def send(d, carry):
        target = lax.rem(me + d, count)
        pltpu.make_async_remote_copy(
            src_ref=x_ref.at[target],
            dst_ref=slots.at[me],
            send_sem=send_sem.at[target],
            recv_sem=recv_sem.at[me],
            device_id={"pan": target},
            device_id_type=pl.DeviceIdType.MESH,
        ).start()
        return carry

    barrier = pltpu.get_barrier_semaphore()

    def knock(d, carry):
        pl.semaphore_signal(barrier, inc=1, device_id={"pan": lax.rem(me + d, count)}, device_id_type=pl.DeviceIdType.MESH)
        return carry

    lax.fori_loop(1, count, knock, 0)
    pl.semaphore_wait(barrier, count - 1)
    lax.fori_loop(1, count, send, 0)
    total = x_ref[me]

    def gather(d, total):
        source = lax.rem(me + count - d, count)
        pltpu.make_async_remote_copy(
            src_ref=x_ref.at[source],
            dst_ref=slots.at[source],
            send_sem=send_sem.at[source],
            recv_sem=recv_sem.at[source],
            device_id={"pan": source},
            device_id_type=pl.DeviceIdType.MESH,
        ).wait_recv()
        return total + slots[source]

    total = lax.fori_loop(1, count, gather, total)

    def drain(d, carry):
        target = lax.rem(me + d, count)
        pltpu.make_async_remote_copy(
            src_ref=x_ref.at[target],
            dst_ref=slots.at[me],
            send_sem=send_sem.at[target],
            recv_sem=recv_sem.at[me],
            device_id={"pan": target},
            device_id_type=pl.DeviceIdType.MESH,
        ).wait_send()
        return carry

    lax.fori_loop(1, count, drain, 0)
    out_ref[...] = total


def exchange_sum(data):
    count = data.shape[0]
    return pl.pallas_call(
        exchange_kernel,
        out_shape=jax.ShapeDtypeStruct(data.shape[1:], data.dtype),
        in_specs=[pl.BlockSpec(memory_space=pltpu.VMEM)],
        out_specs=pl.BlockSpec(memory_space=pltpu.VMEM),
        scratch_shapes=[
            pltpu.VMEM(data.shape, data.dtype),
            pltpu.SemaphoreType.DMA((count,)),
            pltpu.SemaphoreType.DMA((count,)),
        ],
        compiler_params=pltpu.CompilerParams(collective_id=0, has_side_effects=True),
    )(data)


def halving_sum(data, axis, bit_order):
    count = data.shape[0]
    levels = count.bit_length() - 1
    me = lax.axis_index(axis)
    data = data.reshape((2,) * levels + data.shape[1:])
    remaining = list(range(levels - 1, -1, -1))
    for bit in bit_order:
        dim = remaining.index(bit)
        mine = (me >> bit) & 1
        low = lax.index_in_dim(data, 0, dim, keepdims=False)
        high = lax.index_in_dim(data, 1, dim, keepdims=False)
        keep = jnp.where(mine == 1, high, low)
        send = jnp.where(mine == 1, low, high)
        pairs = [(p, p ^ (1 << bit)) for p in range(count)]
        data = keep + lax.ppermute(send, axis, pairs)
        remaining.pop(dim)
    return data


def solution(mesh):
    return jax.shard_map(
        per_device,
        mesh=mesh,
        in_specs=(
            P("pan", None, "obs", None),
            P("pan", None, "obs"),
            P(None, "obs"),
            P(None, "pan", "obs"),
            P(None, "pan", "obs"),
            P(),
        ),
        out_specs=P("pan", "obs"),
        check_vma=False,
    )
```

```python
import functools
import math

import jax
import jax.numpy as jnp
from jax import lax
from jax.experimental import pallas as pl
from jax.experimental.pallas import tpu as pltpu
from jax.sharding import PartitionSpec as P

MAXD = 127
OBLK = 128
PBLK = 128


def fwh_kernel(bins_ref, me_ref, obs_ref, place_ref, frac_ref, src_ref, out_ref, *, amplitude, panel_blocks, window, bins_total):
    ob = pl.program_id(0)
    here = obs_ref[...].T
    acc = jnp.zeros((OBLK, bins_total), jnp.float32)
    pad = jnp.zeros((OBLK, bins_total - window), jnp.float32)
    for pb in range(panel_blocks):
        cols = slice(pb * PBLK, (pb + 1) * PBLK)
        seps = [here[:, c : c + 1] - place_ref[c : c + 1, cols] for c in range(3)]
        dist_sq = seps[0] * seps[0] + seps[1] * seps[1] + seps[2] * seps[2]
        inverse = 1.0 / dist_sq
        parts = [amplitude / jnp.sqrt(dist_sq)] + [(amplitude * sep) * inverse for sep in seps]
        weight = frac_ref[:, cols].astype(jnp.float32)
        rest = 1.0 - weight
        lo_w = jnp.concatenate([(part * rest).astype(jnp.bfloat16) for part in parts], axis=1)
        hi_w = jnp.concatenate([(part * weight).astype(jnp.bfloat16) for part in parts], axis=1)
        src = src_ref[:, cols, :].reshape(4 * PBLK, src_ref.shape[2])
        low = jnp.dot(lo_w, src, preferred_element_type=jnp.float32)
        high = jnp.dot(hi_w, src, preferred_element_type=jnp.float32)
        shift = bins_ref[0, pb, ob]
        acc = acc + pltpu.roll(jnp.concatenate([low, pad], axis=1), shift, 1)
        acc = acc + pltpu.roll(jnp.concatenate([high, pad], axis=1), shift + 1, 1)
    out_ref[...] = acc.T


def per_device(sources, panel_places, observer_places, fraction, delay_bins, segment_owner):
    local_panels = sources.shape[2]
    window = sources.shape[3]
    bins_total = window + MAXD + 1
    amplitude = 60.0 / math.sqrt(local_panels * lax.axis_size("obs") * lax.axis_size("pan"))
    panel_blocks = local_panels // PBLK
    obs_count = lax.axis_size("obs")
    obs_me = lax.axis_index("obs")
    arrived = [observer_places] + [
        lax.ppermute(observer_places, "obs", [(p, p ^ k) for p in range(obs_count)]) for k in range(1, obs_count)
    ]
    blocks = []
    for q in range(obs_count):
        block = arrived[0]
        for k in range(1, obs_count):
            block = jnp.where((obs_me ^ k) == q, arrived[k], block)
        blocks.append(block)
    every_obs = jnp.concatenate(blocks, axis=1)
    obs_total = every_obs.shape[1]
    obs_blocks = obs_total // OBLK
    kernel = functools.partial(fwh_kernel, amplitude=amplitude, panel_blocks=panel_blocks, window=window, bins_total=bins_total)
    grid_spec = pltpu.PrefetchScalarGridSpec(
        num_scalar_prefetch=2,
        grid=(obs_blocks,),
        in_specs=[
            pl.BlockSpec((3, OBLK), lambda i, b, m: (0, i)),
            pl.BlockSpec((3, local_panels), lambda i, b, m: (0, 0)),
            pl.BlockSpec((OBLK, local_panels), lambda i, b, m: (i, 0)),
            pl.BlockSpec((4, local_panels, window), lambda i, b, m: (0, 0, 0)),
        ],
        out_specs=pl.BlockSpec((None, bins_total, OBLK), lambda i, b, m: (((i // 2) % 2 + m[0]) % 2 * 2 + ((i // 4) + m[0] // 2) % 2, 0, i % 2)),
    )
    totals = pl.pallas_call(
        kernel,
        grid_spec=grid_spec,
        out_shape=jax.ShapeDtypeStruct((obs_blocks // 2, bins_total, 2 * OBLK), jnp.float32),
    )(jnp.transpose(delay_bins, (1, 2, 0)), jnp.reshape(obs_me, (1,)).astype(jnp.int32), every_obs, panel_places[0], fraction[:, 0, :], sources[0])
    halves = totals.reshape((2, 2) + totals.shape[1:])
    for bit in (0, 1):
        pairs = [(p, p ^ (1 << bit)) for p in range(4)]
        halves = halves[0] + lax.ppermute(halves[1], "obs", pairs)
    reduced = halves
    segment_count = segment_owner.shape[0]
    seg_len = bins_total // segment_count
    arranged = reduced.reshape(segment_count, seg_len, reduced.shape[1])
    inverse = jnp.argsort(segment_owner)
    arranged = arranged[inverse]
    flat = arranged.reshape(segment_count, 1, seg_len * arranged.shape[2])
    return exchange_sum(flat, seg_len)


def exchange_kernel(x_ref, out_ref, slots, send_sem, recv_sem):
    count = x_ref.shape[0]
    me = lax.axis_index("pan")

    def send(d, carry):
        target = lax.rem(me + d, count)
        pltpu.make_async_remote_copy(
            src_ref=x_ref.at[target],
            dst_ref=slots.at[me],
            send_sem=send_sem.at[target],
            recv_sem=recv_sem.at[me],
            device_id={"pan": target},
            device_id_type=pl.DeviceIdType.MESH,
        ).start()
        return carry

    barrier = pltpu.get_barrier_semaphore()

    def knock(d, carry):
        pl.semaphore_signal(barrier, inc=1, device_id={"pan": lax.rem(me + d, count)}, device_id_type=pl.DeviceIdType.MESH)
        return carry

    lax.fori_loop(1, count, knock, 0)
    pl.semaphore_wait(barrier, count - 1)
    lax.fori_loop(1, count, send, 0)
    total = x_ref[me]

    def gather(d, total):
        source = lax.rem(me + count - d, count)
        pltpu.make_async_remote_copy(
            src_ref=x_ref.at[source],
            dst_ref=slots.at[source],
            send_sem=send_sem.at[source],
            recv_sem=recv_sem.at[source],
            device_id={"pan": source},
            device_id_type=pl.DeviceIdType.MESH,
        ).wait_recv()
        return total + slots[source]

    total = lax.fori_loop(1, count, gather, total)

    def drain(d, carry):
        target = lax.rem(me + d, count)
        pltpu.make_async_remote_copy(
            src_ref=x_ref.at[target],
            dst_ref=slots.at[me],
            send_sem=send_sem.at[target],
            recv_sem=recv_sem.at[me],
            device_id={"pan": target},
            device_id_type=pl.DeviceIdType.MESH,
        ).wait_send()
        return carry

    lax.fori_loop(1, count, drain, 0)
    width = out_ref.shape[1]
    for r in range(out_ref.shape[0]):
        out_ref[r : r + 1, :] = total[:, r * width : (r + 1) * width]


def exchange_sum(data, rows):
    count = data.shape[0]
    return pl.pallas_call(
        exchange_kernel,
        out_shape=jax.ShapeDtypeStruct((rows, data.shape[2] // rows), data.dtype),
        in_specs=[pl.BlockSpec(memory_space=pltpu.VMEM)],
        out_specs=pl.BlockSpec(memory_space=pltpu.VMEM),
        scratch_shapes=[
            pltpu.VMEM(data.shape, data.dtype),
            pltpu.SemaphoreType.DMA((count,)),
            pltpu.SemaphoreType.DMA((count,)),
        ],
        compiler_params=pltpu.CompilerParams(collective_id=0, has_side_effects=True),
    )(data)


def halving_sum(data, axis, bit_order):
    count = data.shape[0]
    levels = count.bit_length() - 1
    me = lax.axis_index(axis)
    data = data.reshape((2,) * levels + data.shape[1:])
    remaining = list(range(levels - 1, -1, -1))
    for bit in bit_order:
        dim = remaining.index(bit)
        mine = (me >> bit) & 1
        low = lax.index_in_dim(data, 0, dim, keepdims=False)
        high = lax.index_in_dim(data, 1, dim, keepdims=False)
        keep = jnp.where(mine == 1, high, low)
        send = jnp.where(mine == 1, low, high)
        pairs = [(p, p ^ (1 << bit)) for p in range(count)]
        data = keep + lax.ppermute(send, axis, pairs)
        remaining.pop(dim)
    return data


def solution(mesh):
    return jax.shard_map(
        per_device,
        mesh=mesh,
        in_specs=(
            P("pan", None, "obs", None),
            P("pan", None, "obs"),
            P(None, "obs"),
            P(None, "pan", "obs"),
            P(None, "pan", "obs"),
            P(),
        ),
        out_specs=P("pan", "obs"),
        check_vma=False,
    )
```

```python
import functools
import math

import jax
import jax.numpy as jnp
from jax import lax
from jax.experimental import pallas as pl
from jax.experimental.pallas import tpu as pltpu
from jax.sharding import PartitionSpec as P

MAXD = 127
OBLK = 128
PBLK = 128


def fwh_kernel(bins_ref, me_ref, obs_ref, place_ref, frac_ref, src_ref, out_ref, *, amplitude, panel_blocks, window, bins_total):
    ob = pl.program_id(0)
    here = obs_ref[...].T
    acc = jnp.zeros((OBLK, bins_total), jnp.float32)
    pad = jnp.zeros((OBLK, bins_total - window), jnp.float32)
    for pb in range(panel_blocks):
        cols = slice(pb * PBLK, (pb + 1) * PBLK)
        seps = [here[:, c : c + 1] - place_ref[c : c + 1, cols] for c in range(3)]
        dist_sq = seps[0] * seps[0] + seps[1] * seps[1] + seps[2] * seps[2]
        inverse = 1.0 / dist_sq
        parts = [amplitude / jnp.sqrt(dist_sq)] + [(amplitude * sep) * inverse for sep in seps]
        weight = frac_ref[:, cols].astype(jnp.float32)
        rest = 1.0 - weight
        lo_w = jnp.concatenate([(part * rest).astype(jnp.bfloat16) for part in parts], axis=1)
        hi_w = jnp.concatenate([(part * weight).astype(jnp.bfloat16) for part in parts], axis=1)
        src = src_ref[:, cols, :].reshape(4 * PBLK, src_ref.shape[2])
        low = jnp.dot(lo_w, src, preferred_element_type=jnp.float32)
        high = jnp.dot(hi_w, src, preferred_element_type=jnp.float32)
        shift = bins_ref[0, pb, ob]
        acc = acc + pltpu.roll(jnp.concatenate([low, pad], axis=1), shift, 1)
        acc = acc + pltpu.roll(jnp.concatenate([high, pad], axis=1), shift + 1, 1)
    out_ref[...] = acc.T


def per_device(sources, panel_places, observer_places, fraction, delay_bins, segment_owner):
    local_panels = sources.shape[2]
    window = sources.shape[3]
    bins_total = window + MAXD + 1
    amplitude = 60.0 / math.sqrt(local_panels * lax.axis_size("obs") * lax.axis_size("pan"))
    panel_blocks = local_panels // PBLK
    obs_count = lax.axis_size("obs")
    obs_me = lax.axis_index("obs")
    arrived = [observer_places] + [
        lax.ppermute(observer_places, "obs", [(p, p ^ k) for p in range(obs_count)]) for k in range(1, obs_count)
    ]
    blocks = []
    for q in range(obs_count):
        block = arrived[0]
        for k in range(1, obs_count):
            block = jnp.where((obs_me ^ k) == q, arrived[k], block)
        blocks.append(block)
    every_obs = jnp.concatenate(blocks, axis=1)
    obs_total = every_obs.shape[1]
    obs_blocks = obs_total // OBLK
    kernel = functools.partial(fwh_kernel, amplitude=amplitude, panel_blocks=panel_blocks, window=window, bins_total=bins_total)
    grid_spec = pltpu.PrefetchScalarGridSpec(
        num_scalar_prefetch=2,
        grid=(obs_blocks,),
        in_specs=[
            pl.BlockSpec((3, OBLK), lambda i, b, m: (0, i)),
            pl.BlockSpec((3, local_panels), lambda i, b, m: (0, 0)),
            pl.BlockSpec((OBLK, local_panels), lambda i, b, m: (i, 0)),
            pl.BlockSpec((4, local_panels, window), lambda i, b, m: (0, 0, 0)),
        ],
        out_specs=pl.BlockSpec((None, bins_total, OBLK), lambda i, b, m: (((i // 2) % 2 + m[0]) % 2 * 2 + ((i // 4) + m[0] // 2) % 2, 0, i % 2)),
    )
    totals = pl.pallas_call(
        kernel,
        grid_spec=grid_spec,
        out_shape=jax.ShapeDtypeStruct((obs_blocks // 2, bins_total, 2 * OBLK), jnp.float32),
    )(jnp.transpose(delay_bins, (1, 2, 0)), jnp.reshape(obs_me, (1,)).astype(jnp.int32), every_obs, panel_places[0], fraction[:, 0, :], sources[0])
    halves = totals.reshape((2, 2) + totals.shape[1:])
    for bit in (0, 1):
        pairs = [(p, p ^ (1 << bit)) for p in range(4)]
        halves = halves[0] + lax.ppermute(halves[1], "obs", pairs)
    reduced = halves
    segment_count = segment_owner.shape[0]
    seg_len = bins_total // segment_count
    arranged = reduced.reshape(segment_count, seg_len, reduced.shape[1])
    inverse = jnp.argsort(segment_owner)
    arranged = arranged[inverse]
    flat = arranged.reshape(segment_count, 1, seg_len * arranged.shape[2])
    return exchange_sum(flat).reshape(seg_len, arranged.shape[2])


def exchange_kernel(x_ref, out_ref, slots, send_sem, recv_sem):
    count = x_ref.shape[0]
    me = lax.axis_index("pan")

    def offset(d):
        return (d % 2 * 2 - 1) * ((d + 1) // 2)

    def send(d, carry):
        target = lax.rem(me + offset(d) + count, count)
        pltpu.make_async_remote_copy(
            src_ref=x_ref.at[target],
            dst_ref=slots.at[me],
            send_sem=send_sem.at[target],
            recv_sem=recv_sem.at[me],
            device_id={"pan": target},
            device_id_type=pl.DeviceIdType.MESH,
        ).start()
        return carry

    barrier = pltpu.get_barrier_semaphore()

    def knock(d, carry):
        pl.semaphore_signal(barrier, inc=1, device_id={"pan": lax.rem(me + d, count)}, device_id_type=pl.DeviceIdType.MESH)
        return carry

    lax.fori_loop(1, count, knock, 0)
    pl.semaphore_wait(barrier, count - 1)
    lax.fori_loop(1, count, send, 0)
    total = x_ref[me]

    def gather(d, total):
        source = lax.rem(me + count - offset(d), count)
        pltpu.make_async_remote_copy(
            src_ref=x_ref.at[source],
            dst_ref=slots.at[source],
            send_sem=send_sem.at[source],
            recv_sem=recv_sem.at[source],
            device_id={"pan": source},
            device_id_type=pl.DeviceIdType.MESH,
        ).wait_recv()
        return total + slots[source]

    total = lax.fori_loop(1, count, gather, total)

    def drain(d, carry):
        target = lax.rem(me + d, count)
        pltpu.make_async_remote_copy(
            src_ref=x_ref.at[target],
            dst_ref=slots.at[me],
            send_sem=send_sem.at[target],
            recv_sem=recv_sem.at[me],
            device_id={"pan": target},
            device_id_type=pl.DeviceIdType.MESH,
        ).wait_send()
        return carry

    lax.fori_loop(1, count, drain, 0)
    out_ref[...] = total


def exchange_sum(data):
    count = data.shape[0]
    return pl.pallas_call(
        exchange_kernel,
        out_shape=jax.ShapeDtypeStruct(data.shape[1:], data.dtype),
        in_specs=[pl.BlockSpec(memory_space=pltpu.VMEM)],
        out_specs=pl.BlockSpec(memory_space=pltpu.VMEM),
        scratch_shapes=[
            pltpu.VMEM(data.shape, data.dtype),
            pltpu.SemaphoreType.DMA((count,)),
            pltpu.SemaphoreType.DMA((count,)),
        ],
        compiler_params=pltpu.CompilerParams(collective_id=0, has_side_effects=True),
    )(data)


def halving_sum(data, axis, bit_order):
    count = data.shape[0]
    levels = count.bit_length() - 1
    me = lax.axis_index(axis)
    data = data.reshape((2,) * levels + data.shape[1:])
    remaining = list(range(levels - 1, -1, -1))
    for bit in bit_order:
        dim = remaining.index(bit)
        mine = (me >> bit) & 1
        low = lax.index_in_dim(data, 0, dim, keepdims=False)
        high = lax.index_in_dim(data, 1, dim, keepdims=False)
        keep = jnp.where(mine == 1, high, low)
        send = jnp.where(mine == 1, low, high)
        pairs = [(p, p ^ (1 << bit)) for p in range(count)]
        data = keep + lax.ppermute(send, axis, pairs)
        remaining.pop(dim)
    return data


def solution(mesh):
    return jax.shard_map(
        per_device,
        mesh=mesh,
        in_specs=(
            P("pan", None, "obs", None),
            P("pan", None, "obs"),
            P(None, "obs"),
            P(None, "pan", "obs"),
            P(None, "pan", "obs"),
            P(),
        ),
        out_specs=P("pan", "obs"),
        check_vma=False,
    )
```
